32 devices in a mesh: rep: 2 (over x), shard: 4 (over y, core), ctx: 4 (over z).
Axes of the slice: x: 2, y: 2, z: 4, core: 2. Of those that a mesh axis runs over, the one named last changes fastest.
Arguments:
- tokens: bfloat16 [16, 256, 1024], P(('rep', 'shard'), 'ctx'), may hold values from -6 to 6
- positions: int32 [16, 256], P(('rep', 'shard')), may hold values from 0 to 255, as said below
- segments: int32 [16, 256], P(('rep', 'shard')), may hold values from 0 to 2, as said below
- cotangent: bfloat16 [16, 256, 1024], P(('rep', 'shard'), 'ctx'), may hold values from -6 to 6
- w_query: bfloat16 [1024, 2048], P(None, ('shard', 'ctx')), may hold values from -0.1875 to 0.1875
- key_weight: bfloat16 [1024, 1024], P(None, ('shard', 'ctx')), may hold values from -0.1875 to 0.1875
- value_weight: bfloat16 [1024, 1024], P(None, ('shard', 'ctx')), may hold values from -0.1875 to 0.1875
- output_weight: bfloat16 [2048, 1024], P(('shard', 'ctx')), may hold values from -0.625 to 0.625
- w_gate: bfloat16 [1024, 3072], P(None, ('shard', 'ctx')), may hold values from -0.1875 to 0.1875
- w_up: bfloat16 [1024, 3072], P(None, ('shard', 'ctx')), may hold values from -0.1875 to 0.1875
- w_down: bfloat16 [3072, 1024], P(('shard', 'ctx')), may hold values from -0.109375 to 0.109375
- norm_gains: bfloat16 [2304], P(('shard', 'ctx')), may hold values from 0.5 to 1.5
Outputs:
- block_out: bfloat16 [16, 256, 1024], P(('rep', 'shard'), 'ctx')
- grad_input: float32 [16, 256, 1024], P(('rep', 'shard'), 'ctx')
- grad_query: float32 [1024, 2048], P(None, ('shard', 'ctx'))
- grad_key: float32 [1024, 1024], P(None, ('shard', 'ctx'))
- grad_value: float32 [1024, 1024], P(None, ('shard', 'ctx'))
- grad_output: float32 [2048, 1024], P(('shard', 'ctx'))
- grad_gate: float32 [1024, 3072], P(None, ('shard', 'ctx'))
- grad_up: float32 [1024, 3072], P(None, ('shard', 'ctx'))
- grad_down: float32 [3072, 1024], P(('shard', 'ctx'))
- grad_gains: float32 [2304], P(('shard', 'ctx'))
The draws below stay inside these ranges and needn't reach their ends.
Inputs may be any that keep to these rules, and one draw needn't show every extreme that they name: In each sequence the stored positions are a permutation of all its positions made of runs of 32 consecutive positions; the two runs held by one index of ctx are the k-th from the start and the k-th from the end of the sequence, with k drawn per sequence. `segments`: ordered by position, a sequence's document numbers never fall, start at 0 and use every number up to 2.
All inputs are finite; a program needn't handle non-finite values.
Results may differ from the reference program's by a relative error of at most 0.02.
Values may be sent and summed in bfloat16 or wider, within the bound.
A program may use at most 192 MiB of HBM per device.

```python
import math
import jax
import jax.numpy as jnp
from jax import lax

MODEL_DIM = 1024
QUERY_HEADS = 16
KEY_VALUE_HEADS = 8
HEAD_DIM = 128
FF = 3072
SPAN = 32
DOCS = 3
SEQ_LEN = 256
BATCH = 16
GAINS = 2304


def layout_tables(key):
    pair_count = SEQ_LEN // (2 * SPAN)
    within = jnp.arange(SPAN, dtype=jnp.int32)

    def one_sequence(sub_key):
        order_key, cut_key = jax.random.split(sub_key)
        span_order = jax.random.permutation(order_key, pair_count).astype(jnp.int32)
        mirrored = 2 * pair_count - 1 - span_order
        span_ids = jnp.stack([span_order, mirrored], axis=1).reshape(2 * pair_count)
        stored = (span_ids[:, None] * SPAN + within[None, :]).reshape(SEQ_LEN)
        cut_all = jax.random.permutation(cut_key, SEQ_LEN - 1).astype(jnp.int32) + 1
        cut_points = cut_all[:DOCS - 1]
        doc_ids = jnp.sum((cut_points[None, :] <= stored[:, None]).astype(jnp.int32), axis=1)
        return (stored, doc_ids.astype(jnp.int32))
    seq_keys = jax.random.split(jax.random.fold_in(key, 7), BATCH)
    return jax.vmap(one_sequence)(seq_keys)


def draw_positions(key, part):
    return layout_tables(key)[0]


def draw_segments(key, part):
    return layout_tables(key)[1]


def level_of(rng, shape, shards, least, largest):
    level, own = 1.0, jax.random.fold_in(rng, 6)
    for axis_at, blocks in shards:
        heights = jnp.exp(jax.random.uniform(jax.random.fold_in(own, axis_at), (blocks,), jnp.float32, least / len(shards), largest / len(shards)))
        level = level * jnp.repeat(heights, shape[axis_at] // blocks).reshape([-1 if axis == axis_at else 1 for axis in range(len(shape))])
    return level


def centred(key, shape, width, limit, pieces=(), kind=jnp.bfloat16):
    array = jax.random.normal(key, shape, jnp.float32) * width
    if len(pieces) > 0:
        array = level_of(key, shape, pieces, -0.22, 0.18) * array
    return jnp.clip(array, min=-limit, max=limit).astype(kind)


def setup_inputs(seed: int = 0) -> dict:
    streams_of = jax.random.split(jax.random.key(seed), 13)
    return {
        "tokens": centred(streams_of[0], (BATCH, SEQ_LEN, MODEL_DIM), 1.0, 6.0, ((0, 8), (1, 4))),
        "positions": draw_positions(jax.random.fold_in(streams_of[12], 71), 0),
        "segments": draw_segments(jax.random.fold_in(streams_of[12], 71), 0),
        "cotangent": centred(streams_of[3], (BATCH, SEQ_LEN, MODEL_DIM), 1.0, 6.0, ((0, 8), (1, 4))),
        "w_query": centred(streams_of[4], (MODEL_DIM, QUERY_HEADS * HEAD_DIM), MODEL_DIM ** -0.5, 0.1875, ((1, 16),)),
        "key_weight": centred(streams_of[5], (MODEL_DIM, KEY_VALUE_HEADS * HEAD_DIM), MODEL_DIM ** -0.5, 0.1875, ((1, 16),)),
        "value_weight": centred(streams_of[6], (MODEL_DIM, KEY_VALUE_HEADS * HEAD_DIM), MODEL_DIM ** -0.5, 0.1875, ((1, 16),)),
        "output_weight": centred(streams_of[7], (QUERY_HEADS * HEAD_DIM, MODEL_DIM), (max(1, QUERY_HEADS * HEAD_DIM * 4 * DOCS // SEQ_LEN)) ** -0.5, 0.625, ((0, 16),)),
        "w_gate": centred(streams_of[8], (MODEL_DIM, FF), MODEL_DIM ** -0.5, 0.1875, ((1, 16),)),
        "w_up": centred(streams_of[9], (MODEL_DIM, FF), MODEL_DIM ** -0.5, 0.1875, ((1, 16),)),
        "w_down": centred(streams_of[10], (FF, MODEL_DIM), FF ** -0.5, 0.109375, ((0, 16),)),
        "norm_gains": jnp.clip(1.0 + 0.1 * jax.random.normal(streams_of[11], (GAINS,), jnp.float32), 0.5, 1.5).astype(jnp.bfloat16),
    }


EPSILON = 1e-06
ROPE_BASE = 1000000.0
HIGH = lax.Precision.HIGHEST

def rms_scale(values_in):
    return lax.rsqrt(lax.optimization_barrier(jnp.mean(values_in * values_in, axis=-1, keepdims=True)) + EPSILON)

def norm_backward(grad_in, values_in, scale_in, gain_in):
    grad_norm = grad_in * gain_in
    unit = values_in * scale_in
    return scale_in * (grad_norm - unit * lax.optimization_barrier(jnp.mean(grad_norm * unit, axis=-1, keepdims=True)))

def rope_tables(position_ids):
    half_dim = HEAD_DIM // 2
    inverse = 1.0 / ROPE_BASE ** (jnp.arange(half_dim, dtype=jnp.float32) * (2.0 / HEAD_DIM))
    angle = position_ids.astype(jnp.float32)[..., None] * inverse
    return (jnp.cos(angle)[:, :, None, :], jnp.sin(angle)[:, :, None, :])

def rotate(values_in, cosine, sine):
    half_dim = values_in.shape[-1] // 2
    first = values_in[..., :half_dim]
    second = values_in[..., half_dim:]
    return jnp.concatenate([first * cosine - second * sine, second * cosine + first * sine], axis=-1)

def rotate_back(grad_in, cosine, sine):
    half_dim = grad_in.shape[-1] // 2
    first = grad_in[..., :half_dim]
    second = grad_in[..., half_dim:]
    return jnp.concatenate([first * cosine + second * sine, second * cosine - first * sine], axis=-1)

def float_product(left, right):
    return jnp.dot(left, right, preferred_element_type=jnp.float32)

def layer_block(tokens, positions, segments, cotangent, weights):
    w_query, key_weight, value_weight, output_weight, w_gate, w_up, w_down, gain_all = weights
    sequence_count, sequence_length, model_width = tokens.shape
    total_rows = sequence_count * sequence_length
    group_width = QUERY_HEADS // KEY_VALUE_HEADS
    score_scale = 1.0 / math.sqrt(HEAD_DIM)
    g_attn = gain_all[:MODEL_DIM]
    g_query = gain_all[MODEL_DIM:MODEL_DIM + HEAD_DIM]
    key_gain = gain_all[MODEL_DIM + HEAD_DIM:MODEL_DIM + 2 * HEAD_DIM]
    g_mlp = gain_all[MODEL_DIM + 2 * HEAD_DIM:]
    x_rows = tokens.reshape(total_rows, MODEL_DIM).astype(jnp.float32)
    scale_in = rms_scale(x_rows)
    normed_input = (x_rows * scale_in * g_attn).astype(jnp.bfloat16)
    query = float_product(normed_input, w_query).reshape(sequence_count, sequence_length, QUERY_HEADS, HEAD_DIM)
    key_rows = float_product(normed_input, key_weight).reshape(sequence_count, sequence_length, KEY_VALUE_HEADS, HEAD_DIM)
    value_rows = float_product(normed_input, value_weight).astype(jnp.bfloat16).reshape(sequence_count, sequence_length, KEY_VALUE_HEADS, HEAD_DIM)
    q_scale = rms_scale(query)
    key_scale = rms_scale(key_rows)
    cosine, sine = rope_tables(positions)
    query_rotated = rotate(query * q_scale * g_query, cosine, sine).astype(jnp.bfloat16)
    k_rot = rotate(key_rows * key_scale * key_gain, cosine, sine).astype(jnp.bfloat16)
    allowed = ((segments[:, :, None] == segments[:, None, :]) & (positions[:, None, :] <= positions[:, :, None]))[:, None, None]
    query_group = query_rotated.reshape(sequence_count, sequence_length, KEY_VALUE_HEADS, group_width, HEAD_DIM).astype(jnp.float32)
    k_float = k_rot.astype(jnp.float32)
    v_float = value_rows.astype(jnp.float32)
    scores = jnp.einsum('bqkgd,bskd->bkgqs', query_group, k_float, precision=HIGH) * score_scale
    exponent = jnp.where(allowed, jnp.exp(scores), 0.0)
    denominator = lax.optimization_barrier(jnp.sum(exponent, axis=-1))
    log_total = jnp.log(denominator)
    probs = (exponent / denominator[..., None]).astype(jnp.bfloat16)
    attention_output = jnp.einsum('bkgqs,bskd->bqkgd', probs.astype(jnp.float32), v_float, precision=HIGH)
    attention_output = attention_output.astype(jnp.bfloat16).reshape(total_rows, QUERY_HEADS * HEAD_DIM)
    mixed_in = x_rows + float_product(attention_output, output_weight)
    scale_mid = rms_scale(mixed_in)
    normed_mid = (mixed_in * scale_mid * g_mlp).astype(jnp.bfloat16)
    gate_pre = float_product(normed_mid, w_gate)
    up_pre = float_product(normed_mid, w_up)
    sigmoid_gate = jax.nn.sigmoid(gate_pre)
    hidden = (gate_pre * sigmoid_gate * up_pre).astype(jnp.bfloat16)
    block_sum = mixed_in + float_product(hidden, w_down)
    block_out = block_sum.astype(jnp.bfloat16).reshape(sequence_count, sequence_length, MODEL_DIM)
    grad_rows = cotangent.reshape(total_rows, MODEL_DIM)
    d_hidden = float_product(grad_rows, w_down.T)
    grad_down = float_product(hidden.T, grad_rows)
    d_gate = (d_hidden * up_pre * sigmoid_gate * (1.0 + gate_pre * (1.0 - sigmoid_gate))).astype(jnp.bfloat16)
    d_up = (d_hidden * gate_pre * sigmoid_gate).astype(jnp.bfloat16)
    grad_gate = float_product(normed_mid.T, d_gate)
    grad_up = float_product(normed_mid.T, d_up)
    d_mid = float_product(d_gate, w_gate.T) + float_product(d_up, w_up.T)
    dg_mlp = lax.optimization_barrier(jnp.sum(d_mid * mixed_in * scale_mid, axis=0))
    d_resid = grad_rows.astype(jnp.float32) + norm_backward(d_mid, mixed_in, scale_mid, g_mlp)
    residual_gradient_bfloat = d_resid.astype(jnp.bfloat16)
    grad_output = float_product(attention_output.T, residual_gradient_bfloat)
    attention_gradient = float_product(residual_gradient_bfloat, output_weight.T).astype(jnp.bfloat16).reshape(sequence_count, sequence_length, KEY_VALUE_HEADS, group_width, HEAD_DIM)
    d_att_float = attention_gradient.astype(jnp.float32)
    attention_float = attention_output.reshape(sequence_count, sequence_length, KEY_VALUE_HEADS, group_width, HEAD_DIM).astype(jnp.float32)
    row_delta = jnp.transpose(lax.optimization_barrier(jnp.sum(d_att_float * attention_float, axis=-1)), (0, 2, 3, 1))
    probs_back = jnp.where(allowed, jnp.exp(scores - log_total[..., None]), 0.0)
    probs_round = probs_back.astype(jnp.bfloat16).astype(jnp.float32)
    values_gradient = jnp.einsum('bkgqs,bqkgd->bskd', probs_round, d_att_float, precision=HIGH)
    d_probs = jnp.einsum('bqkgd,bskd->bkgqs', d_att_float, v_float, precision=HIGH)
    d_scores = (probs_back * (d_probs - row_delta[..., None])).astype(jnp.bfloat16).astype(jnp.float32)
    d_qrot = jnp.einsum('bkgqs,bskd->bqkgd', d_scores, k_float, precision=HIGH) * score_scale
    d_krot = jnp.einsum('bkgqs,bqkgd->bskd', d_scores, query_group, precision=HIGH) * score_scale
    d_qn = rotate_back(d_qrot.reshape(sequence_count, sequence_length, QUERY_HEADS, HEAD_DIM), cosine, sine)
    normed_key_gradient = rotate_back(d_krot, cosine, sine)
    dg_query = lax.optimization_barrier(jnp.sum(d_qn * query * q_scale, axis=(0, 1, 2)))
    dg_key = lax.optimization_barrier(jnp.sum(normed_key_gradient * key_rows * key_scale, axis=(0, 1, 2)))
    d_query = norm_backward(d_qn, query, q_scale, g_query).astype(jnp.bfloat16).reshape(total_rows, QUERY_HEADS * HEAD_DIM)
    key_gradient = norm_backward(normed_key_gradient, key_rows, key_scale, key_gain).astype(jnp.bfloat16).reshape(total_rows, KEY_VALUE_HEADS * HEAD_DIM)
    value_gradient = values_gradient.astype(jnp.bfloat16).reshape(total_rows, KEY_VALUE_HEADS * HEAD_DIM)
    grad_query = float_product(normed_input.T, d_query)
    grad_key = float_product(normed_input.T, key_gradient)
    grad_value = float_product(normed_input.T, value_gradient)
    d_in = float_product(d_query, w_query.T) + float_product(key_gradient, key_weight.T) + float_product(value_gradient, value_weight.T)
    dg_attn = lax.optimization_barrier(jnp.sum(d_in * x_rows * scale_in, axis=0))
    grad_input = (d_resid + norm_backward(d_in, x_rows, scale_in, g_attn)).reshape(sequence_count, sequence_length, MODEL_DIM)
    grad_gains = jnp.concatenate([dg_attn, dg_query, dg_key, dg_mlp])
    grads = (grad_query, grad_key, grad_value, grad_output, grad_gate, grad_up, grad_down, grad_gains)
    return (block_out, grad_input, grads)

def reference(tokens, positions, segments, cotangent, w_query, key_weight, value_weight, output_weight, w_gate, w_up, w_down, norm_gains):
    group_count = math.gcd(BATCH, max(1, 4096 // SEQ_LEN))
    step_count = BATCH // group_count
    weights = (w_query, key_weight, value_weight, output_weight, w_gate, w_up, w_down, norm_gains.astype(jnp.float32))

    def split_groups(array_in):
        return array_in.reshape((step_count, group_count) + array_in.shape[1:])
    initial = tuple((jnp.zeros(wt.shape, jnp.float32) for wt in weights[:7])) + (jnp.zeros((GAINS,), jnp.float32),)

    def advance(carry, item):
        block_out, grad_input, grads = layer_block(item[0], item[1], item[2], item[3], weights)
        return (tuple((c_old + g_new for c_old, g_new in zip(carry, grads))), (block_out, grad_input))
    carry, stacked = lax.scan(advance, initial, (split_groups(tokens), split_groups(positions), split_groups(segments), split_groups(cotangent)))
    block_out = stacked[0].reshape(BATCH, SEQ_LEN, MODEL_DIM)
    grad_input = stacked[1].reshape(BATCH, SEQ_LEN, MODEL_DIM)
    return (block_out, grad_input, carry[0], carry[1], carry[2], carry[3], carry[4], carry[5], carry[6], carry[7])
```

```python
import functools
import math

import jax
import jax.numpy as jnp
from jax import lax
from jax.experimental import pallas as pl
from jax.experimental.pallas import tpu as pltpu
from jax.sharding import PartitionSpec as P

QUERY_HEADS = 16
KEY_VALUE_HEADS = 8
HEAD_DIM = 128

MESH = pl.DeviceIdType.MESH

EPSILON = 1e-06
ROPE_BASE = 1000000.0


def rms_scale(values_in):
    return lax.rsqrt(jnp.mean(values_in * values_in, axis=-1, keepdims=True) + EPSILON)


def norm_backward(grad_in, values_in, scale_in, gain_in):
    grad_norm = grad_in * gain_in
    unit = values_in * scale_in
    return scale_in * (grad_norm - unit * jnp.mean(grad_norm * unit, axis=-1, keepdims=True))


def rope_tables(position_ids):
    half_dim = HEAD_DIM // 2
    inverse = 1.0 / ROPE_BASE ** (jnp.arange(half_dim, dtype=jnp.float32) * (2.0 / HEAD_DIM))
    angle = position_ids.astype(jnp.float32)[..., None] * inverse
    return (jnp.cos(angle)[:, :, None, :], jnp.sin(angle)[:, :, None, :])


def rotate(values_in, cosine, sine):
    half_dim = values_in.shape[-1] // 2
    first = values_in[..., :half_dim]
    second = values_in[..., half_dim:]
    return jnp.concatenate(
        [first * cosine - second * sine, second * cosine + first * sine], axis=-1
    )


def rotate_back(grad_in, cosine, sine):
    half_dim = grad_in.shape[-1] // 2
    first = grad_in[..., :half_dim]
    second = grad_in[..., half_dim:]
    return jnp.concatenate(
        [first * cosine + second * sine, second * cosine - first * sine], axis=-1
    )


def float_product(left, right):
    return jnp.dot(left, right, preferred_element_type=jnp.float32)


def against_rows(left, right):
    return lax.dot_general(
        left, right, (((1,), (1,)), ((), ())), preferred_element_type=jnp.float32
    )


def over_tokens(left, right):
    return lax.dot_general(
        left, right, (((0,), (0,)), ((), ())), preferred_element_type=jnp.float32
    )


def body(
    tokens,
    positions,
    segments,
    cotangent,
    w_query,
    key_weight,
    value_weight,
    output_weight,
    w_gate,
    w_up,
    w_down,
    norm_gains,
):
    sequence_count, local_length, model_width = tokens.shape
    total_rows = sequence_count * local_length
    group_width = QUERY_HEADS // KEY_VALUE_HEADS
    score_scale = 1.0 / math.sqrt(HEAD_DIM)
    local_start = lax.axis_index("ctx") * local_length
    local_pos = lax.dynamic_slice_in_dim(positions, local_start, local_length, 1)
    local_seg = lax.dynamic_slice_in_dim(segments, local_start, local_length, 1)
    wq_full, full_key_weight, full_value_weight, wo_full, gains_full = (
        lax.all_gather(w_query, ("shard", "ctx"), axis=1, tiled=True),
        lax.all_gather(key_weight, ("shard", "ctx"), axis=1, tiled=True),
        lax.all_gather(value_weight, ("shard", "ctx"), axis=1, tiled=True),
        lax.all_gather(output_weight, ("shard", "ctx"), axis=0, tiled=True),
        lax.all_gather(norm_gains, ("shard", "ctx"), axis=0, tiled=True),
    )
    gain_all = gains_full.astype(jnp.float32)
    g_attn = gain_all[:model_width]
    g_query = gain_all[model_width : model_width + HEAD_DIM]
    key_gain = gain_all[model_width + HEAD_DIM : model_width + 2 * HEAD_DIM]
    g_mlp = gain_all[model_width + 2 * HEAD_DIM :]
    x_rows = tokens.reshape(total_rows, model_width).astype(jnp.float32)
    scale_in = rms_scale(x_rows)
    normed_input = (x_rows * scale_in * g_attn).astype(jnp.bfloat16)
    query = float_product(normed_input, wq_full).reshape(
        sequence_count, local_length, QUERY_HEADS, HEAD_DIM
    )
    key_rows = float_product(normed_input, full_key_weight).reshape(
        sequence_count, local_length, KEY_VALUE_HEADS, HEAD_DIM
    )
    value_rows = (
        float_product(normed_input, full_value_weight)
        .astype(jnp.bfloat16)
        .reshape(sequence_count, local_length, KEY_VALUE_HEADS, HEAD_DIM)
    )
    q_scale = rms_scale(query)
    key_scale = rms_scale(key_rows)
    cosine, sine = rope_tables(local_pos)
    query_rotated = rotate(query * q_scale * g_query, cosine, sine).astype(jnp.bfloat16)
    k_rot = rotate(key_rows * key_scale * key_gain, cosine, sine).astype(jnp.bfloat16)
    keys_all, values_all = (
        lax.all_gather(k_rot, "ctx", axis=1, tiled=True),
        lax.all_gather(value_rows, "ctx", axis=1, tiled=True),
    )
    allowed = (
        (local_seg[:, :, None] == segments[:, None, :])
        & (positions[:, None, :] <= local_pos[:, :, None])
    )[:, None, None]
    query_group = query_rotated.reshape(
        sequence_count, local_length, KEY_VALUE_HEADS, group_width, HEAD_DIM
    )
    scores = (
        jnp.einsum("bqkgd,bskd->bkgqs", query_group, keys_all, preferred_element_type=jnp.float32)
        * score_scale
    )
    exponent = jnp.where(allowed, jnp.exp(scores), 0.0)
    denominator = jnp.sum(exponent, axis=-1)
    log_total = jnp.log(denominator)
    probs = (exponent / denominator[..., None]).astype(jnp.bfloat16)
    attention_output = jnp.einsum(
        "bkgqs,bskd->bqkgd", probs, values_all, preferred_element_type=jnp.float32
    )
    attention_output = attention_output.astype(jnp.bfloat16).reshape(
        total_rows, QUERY_HEADS * HEAD_DIM
    )
    mixed_in = x_rows + float_product(attention_output, wo_full)
    scale_mid = rms_scale(mixed_in)
    normed_mid = (mixed_in * scale_mid * g_mlp).astype(jnp.bfloat16)
    wg_full, wu_full, wd_full = (
        lax.all_gather(w_gate, ("shard", "ctx"), axis=1, tiled=True),
        lax.all_gather(w_up, ("shard", "ctx"), axis=1, tiled=True),
        lax.all_gather(w_down, ("shard", "ctx"), axis=0, tiled=True),
    )
    gate_pre = float_product(normed_mid, wg_full)
    up_pre = float_product(normed_mid, wu_full)
    sigmoid_gate = jax.nn.sigmoid(gate_pre)
    hidden = (gate_pre * sigmoid_gate * up_pre).astype(jnp.bfloat16)
    block_sum = mixed_in + float_product(hidden, wd_full)
    block_out = block_sum.astype(jnp.bfloat16).reshape(sequence_count, local_length, model_width)
    grad_rows = cotangent.reshape(total_rows, model_width)
    d_hidden = against_rows(grad_rows, wd_full)
    grad_down = over_tokens(hidden, grad_rows)
    d_gate = (d_hidden * up_pre * sigmoid_gate * (1.0 + gate_pre * (1.0 - sigmoid_gate))).astype(
        jnp.bfloat16
    )
    d_up = (d_hidden * gate_pre * sigmoid_gate).astype(jnp.bfloat16)
    grad_gate = over_tokens(normed_mid, d_gate)
    grad_up = over_tokens(normed_mid, d_up)
    owned_gate, owned_up, owned_down = (
        lax.psum_scatter(grad_gate, ("shard", "ctx"), scatter_dimension=1, tiled=True),
        lax.psum_scatter(grad_up, ("shard", "ctx"), scatter_dimension=1, tiled=True),
        lax.psum_scatter(grad_down, ("shard", "ctx"), scatter_dimension=0, tiled=True),
    )
    total_gate, total_up, total_down = (
        lax.psum(owned_gate.astype(jnp.bfloat16), "rep").astype(jnp.float32),
        lax.psum(owned_up.astype(jnp.bfloat16), "rep").astype(jnp.float32),
        lax.psum(owned_down.astype(jnp.bfloat16), "rep").astype(jnp.float32),
    )
    d_mid = against_rows(d_gate, wg_full) + against_rows(d_up, wu_full)
    dg_mlp = jnp.sum(d_mid * mixed_in * scale_mid, axis=0)
    d_resid = grad_rows.astype(jnp.float32) + norm_backward(d_mid, mixed_in, scale_mid, g_mlp)
    residual_gradient_bfloat = d_resid.astype(jnp.bfloat16)
    grad_output = over_tokens(attention_output, residual_gradient_bfloat)
    attention_gradient = (
        against_rows(residual_gradient_bfloat, wo_full)
        .astype(jnp.bfloat16)
        .reshape(sequence_count, local_length, KEY_VALUE_HEADS, group_width, HEAD_DIM)
    )
    attention_heads = attention_output.reshape(
        sequence_count, local_length, KEY_VALUE_HEADS, group_width, HEAD_DIM
    )
    row_delta = jnp.sum(
        attention_gradient.astype(jnp.float32) * attention_heads.astype(jnp.float32), axis=-1
    )
    row_delta = jnp.transpose(row_delta, (0, 2, 3, 1))
    scores_again = (
        jnp.einsum("bqkgd,bskd->bkgqs", query_group, keys_all, preferred_element_type=jnp.float32)
        * score_scale
    )
    probs_back = jnp.where(allowed, jnp.exp(scores_again - log_total[..., None]), 0.0)
    probs_round = probs_back.astype(jnp.bfloat16)
    values_gradient = jnp.einsum(
        "bkgqs,bqkgd->bskd", probs_round, attention_gradient, preferred_element_type=jnp.float32
    )
    d_probs = jnp.einsum(
        "bqkgd,bskd->bkgqs", attention_gradient, values_all, preferred_element_type=jnp.float32
    )
    d_scores = (probs_back * (d_probs - row_delta[..., None])).astype(jnp.bfloat16)
    d_qrot = (
        jnp.einsum("bkgqs,bskd->bqkgd", d_scores, keys_all, preferred_element_type=jnp.float32)
        * score_scale
    )
    d_krot = (
        jnp.einsum("bkgqs,bqkgd->bskd", d_scores, query_group, preferred_element_type=jnp.float32)
        * score_scale
    )
    d_keys, value_rows_gradient = (
        lax.psum_scatter(
            d_krot.astype(jnp.bfloat16), "ctx", scatter_dimension=1, tiled=True
        ).astype(jnp.float32),
        lax.psum_scatter(
            values_gradient.astype(jnp.bfloat16), "ctx", scatter_dimension=1, tiled=True
        ).astype(jnp.float32),
    )
    d_qn = rotate_back(
        d_qrot.reshape(sequence_count, local_length, QUERY_HEADS, HEAD_DIM), cosine, sine
    )
    normed_key_gradient = rotate_back(d_keys, cosine, sine)
    dg_query = jnp.sum(d_qn * query * q_scale, axis=(0, 1, 2))
    dg_key = jnp.sum(normed_key_gradient * key_rows * key_scale, axis=(0, 1, 2))
    d_query = (
        norm_backward(d_qn, query, q_scale, g_query)
        .astype(jnp.bfloat16)
        .reshape(total_rows, QUERY_HEADS * HEAD_DIM)
    )
    key_gradient = (
        norm_backward(normed_key_gradient, key_rows, key_scale, key_gain)
        .astype(jnp.bfloat16)
        .reshape(total_rows, KEY_VALUE_HEADS * HEAD_DIM)
    )
    value_gradient = value_rows_gradient.astype(jnp.bfloat16).reshape(
        total_rows, KEY_VALUE_HEADS * HEAD_DIM
    )
    grad_query = over_tokens(normed_input, d_query)
    grad_key = over_tokens(normed_input, key_gradient)
    grad_value = over_tokens(normed_input, value_gradient)
    d_in = (
        against_rows(d_query, wq_full)
        + against_rows(key_gradient, full_key_weight)
        + against_rows(value_gradient, full_value_weight)
    )
    dg_attn = jnp.sum(d_in * x_rows * scale_in, axis=0)
    grad_input = (d_resid + norm_backward(d_in, x_rows, scale_in, g_attn)).reshape(
        sequence_count, local_length, model_width
    )
    grad_gains = jnp.concatenate([dg_attn, dg_query, dg_key, dg_mlp])
    owned_query, owned_key, owned_value, owned_output, owned_gains = (
        lax.psum_scatter(grad_query, ("shard", "ctx"), scatter_dimension=1, tiled=True),
        lax.psum_scatter(grad_key, ("shard", "ctx"), scatter_dimension=1, tiled=True),
        lax.psum_scatter(grad_value, ("shard", "ctx"), scatter_dimension=1, tiled=True),
        lax.psum_scatter(grad_output, ("shard", "ctx"), scatter_dimension=0, tiled=True),
        lax.psum_scatter(grad_gains, ("shard", "ctx"), scatter_dimension=0, tiled=True),
    )
    total_query, total_key, total_value, total_output, total_gains = (
        lax.psum(owned_query.astype(jnp.bfloat16), "rep").astype(jnp.float32),
        lax.psum(owned_key.astype(jnp.bfloat16), "rep").astype(jnp.float32),
        lax.psum(owned_value.astype(jnp.bfloat16), "rep").astype(jnp.float32),
        lax.psum(owned_output.astype(jnp.bfloat16), "rep").astype(jnp.float32),
        lax.psum(owned_gains.astype(jnp.bfloat16), "rep").astype(jnp.float32),
    )
    return (
        block_out,
        grad_input,
        total_query,
        total_key,
        total_value,
        total_output,
        total_gate,
        total_up,
        total_down,
        total_gains,
    )


def row_plan(head_half, ff):
    sizes = (
        ("q", HEAD_DIM, HEAD_DIM),
        ("k", head_half, HEAD_DIM),
        ("v", head_half, HEAD_DIM),
        ("o", HEAD_DIM, HEAD_DIM),
        ("g", ff, ff),
        ("u", ff, ff),
        ("d", ff, ff),
    )
    plan, own, full = {}, 0, 0
    for name, own_rows, block_rows in sizes:
        plan[name] = (own, own_rows, full, block_rows)
        own, full = own + own_rows, full + 4 * block_rows
    return plan, own, full


def plain(left, right):
    return lax.dot_general(left, right, (((1,), (0,)), ((), ())), preferred_element_type=jnp.float32)


def swap_halves(values_in):
    return pltpu.roll(values_in, values_in.shape[-1] // 2, 1)


def rows(start, size, step):
    return pl.ds(pl.multiple_of(start, step), size)


def layer_kernel(
    plan,
    tok,
    cot,
    wst,
    gain_in,
    mask,
    cosine,
    sine,
    block_out,
    grad_in,
    grad_w,
    gain_out,
    x_all,
    c_all,
    nx,
    nm,
    res,
    own_mid,
    own_res,
    wb,
    qf,
    kf,
    qr,
    kr,
    vb,
    prob,
    att,
    hid,
    dga,
    dup,
    dqb,
    dkb,
    dvb,
    mixed,
    dres,
    part_a,
    part_b,
    got_a,
    got_b,
    got_c,
    got_d,
    gz,
    gsum,
    gz_s,
    gfull,
    dgt,
    dz,
    dsum,
    dz_s,
    dtot,
    dz_x,
    gb,
    rk,
    hs,
    ry,
    kvh,
    kvr,
    xo,
    rx,
    send_sem,
    recv_sem,
):
    sequences, span, width = tok.shape
    ctx = lax.axis_size("ctx")
    length = span * ctx
    heads = 4
    scale = 1.0 / math.sqrt(HEAD_DIM)
    r, s, c = lax.axis_index("rep"), lax.axis_index("shard"), lax.axis_index("ctx")
    core, side = s % 2, s // 2
    sib, opp = s + 1 - 2 * core, (s + 2) % 4
    dia = (sib + 2) % 4
    mine, theirs = core * 2 + side, core * 2 + 1 - side
    half = c % 2
    partner = c + 1 - 2 * half
    steps = list(range(1, ctx))
    sends = []

    def send(src, dst, **where):
        at = len(sends)
        copy = pltpu.make_async_remote_copy(
            src_ref=src,
            dst_ref=dst,
            send_sem=send_sem.at[at],
            recv_sem=recv_sem.at[at],
            device_id=where,
            device_id_type=MESH,
        )
        copy.start()
        sends.append(copy)
        return copy

    def arrive(copies):
        for copy in copies:
            copy.wait_recv()

    def around(d):
        return lax.rem(c + d, ctx)

    def gather(src, dst):
        return [send(src, dst.at[:, c], ctx=around(d)) for d in steps]

    def scatter(src, dst):
        return [send(src.at[around(d)], dst.at[d - 1], ctx=around(d)) for d in steps]

    def keep(src, dst):
        for b in range(sequences):
            dst[b, c] = src[b]

    def block(name, at):
        _, _, off, size = plan[name]
        return rows(off + at * size, size, 64)

    def spread(name, src):
        own = block(name, mine)
        return send(src, wb.at[own], shard=opp), send(src, wb.at[own], shard=sib)

    def pass_on(name):
        got = block(name, theirs)
        return send(wb.at[got], wb.at[got], shard=sib)

    def own_rows(name):
        off, size = plan[name][:2]
        return pl.ds(off, size)

    def matrix(name):
        _, _, off, size = plan[name]
        return wb[pl.ds(off, 4 * size), :]

    def whole(ref, b):
        return ref[b].reshape(length, width)

    def split(values_in, dst, b):
        for j in range(ctx):
            dst[j, b] = values_in[j * span : (j + 1) * span].astype(jnp.bfloat16)

    def collect(src, got, b):
        total = src[c, b].astype(jnp.float32)
        for d in steps:
            total = total + got[d - 1, b].astype(jnp.float32)
        return total

    barrier = pltpu.get_barrier_semaphore()
    peers = [{"ctx": around(d)} for d in steps]
    peers += [{"shard": sib}, {"shard": opp}, {"shard": dia}, {"rep": 1 - r}]
    for peer in peers:
        pl.semaphore_signal(barrier, inc=1, device_id=peer, device_id_type=MESH)
    pl.semaphore_wait(barrier, len(peers))

    head_half = plan["k"][1]
    lanes = [
        rows(plan[name][2] + mine * HEAD_DIM + half * head_half, head_half, 64) for name in "kv"
    ]
    kv_in = [send(wst.at[own_rows(n)], wb.at[at], ctx=partner) for n, at in zip("kv", lanes)]
    gains = [send(gain_in, gz.at[d - 1], ctx=around(d)) for d in steps]
    tok_in = gather(tok, x_all)
    spreads = {"q": spread("q", wst.at[own_rows("q")])}
    for n, at in zip("kv", lanes):
        wb[at, :] = wst[own_rows(n), :]
    for n in "qogud":
        wb[block(n, mine), :] = wst[own_rows(n), :]
    keep(tok, x_all)
    keep(cot, c_all)
    arrive(kv_in)
    for n in "kv":
        spreads[n] = spread(n, wb.at[block(n, mine)])
    for n in "ogud":
        spreads[n] = spread(n, wst.at[own_rows(n)])
    arrive(gains)
    total = gain_in[...]
    for d in steps:
        total = total + gz[d - 1]
    gsum[...] = total
    gains = [send(gsum, gz_s.at[i], shard=p) for i, p in enumerate((sib, opp, dia))]
    arrive(tok_in)
    cot_in = gather(cot, c_all)
    arrive(gains)
    gfull[...] = gsum[...] + gz_s[0] + gz_s[1] + gz_s[2]
    g_attn = gfull[0:1, :]
    g_mlp = gfull[1:2, :]
    g_query = gfull[2:3, :HEAD_DIM]
    g_key = gfull[2:3, HEAD_DIM : 2 * HEAD_DIM]

    def norm_rows(i, carry):
        b, j = i // ctx, i % ctx
        x = x_all[b, j].astype(jnp.float32)
        nx[b, j] = (x * rms_scale(x) * g_attn).astype(jnp.bfloat16)
        return carry

    lax.fori_loop(0, sequences * ctx, norm_rows, 0)

    passed = {}
    for n in "qkv":
        arrive([spreads[n][0]])
        passed[n] = pass_on(n)
    for n in "qkv":
        arrive([spreads[n][1], passed[n]])

    def attend(b, carry):
        x = whole(nx, b)
        query = against_rows(x, matrix("q"))
        key = against_rows(x, matrix("k"))
        value = against_rows(x, matrix("v")).astype(jnp.bfloat16)
        cos_b, sin_b, allowed = cosine[b], sine[b], mask[b] > 0.5
        for h in range(heads):
            at = slice(h * HEAD_DIM, (h + 1) * HEAD_DIM)
            q, k, v = query[:, at], key[:, at], value[:, at]
            qn = q * rms_scale(q) * g_query
            kn = k * rms_scale(k) * g_key
            q_rot = (qn * cos_b + swap_halves(qn) * sin_b).astype(jnp.bfloat16)
            k_rot = (kn * cos_b + swap_halves(kn) * sin_b).astype(jnp.bfloat16)
            qf[b, h], kf[b, h] = q, k
            qr[b, h], kr[b, h], vb[b, h] = q_rot, k_rot, v
            scores = against_rows(q_rot, k_rot) * scale
            exponent = jnp.where(allowed, jnp.exp(scores), 0.0)
            p = exponent / jnp.sum(exponent, axis=-1, keepdims=True)
            prob[b, h] = p
            att[b, :, at] = plain(p.astype(jnp.bfloat16), v).astype(jnp.bfloat16)
        return carry

    lax.fori_loop(0, sequences, attend, 0)

    arrive([spreads["o"][0]])
    passed["o"] = pass_on("o")
    arrive([spreads["o"][1], passed["o"]])

    def project(b, carry):
        split(plain(att[b], matrix("o")), part_a, b)
        return carry

    lax.fori_loop(0, sequences, project, 0)
    copies = scatter(part_a, got_a)
    for n in "gud":
        arrive([spreads[n][0]])
        passed[n] = pass_on(n)
    arrive(copies)
    for b in range(sequences):
        m = tok[b].astype(jnp.float32) + collect(part_a, got_a, b)
        mixed[b] = m
        own_mid[b] = (m * rms_scale(m) * g_mlp).astype(jnp.bfloat16)
    mid_in = gather(own_mid, nm)
    keep(own_mid, nm)
    for n in "gud":
        arrive([spreads[n][1], passed[n]])
    arrive(cot_in)
    arrive(mid_in)

    def feed(b, carry):
        n, ct = whole(nm, b), whole(c_all, b)
        gate = against_rows(n, matrix("g"))
        up = against_rows(n, matrix("u"))
        d_hidden = against_rows(ct, matrix("d"))
        sig = jax.nn.sigmoid(gate)
        hid[b] = (gate * sig * up).astype(jnp.bfloat16)
        d_gate = (d_hidden * up * sig * (1.0 + gate * (1.0 - sig))).astype(jnp.bfloat16)
        d_up = (d_hidden * gate * sig).astype(jnp.bfloat16)
        dga[b], dup[b] = d_gate, d_up
        split(plain(d_gate, matrix("g")) + plain(d_up, matrix("u")), part_b, b)
        return carry

    lax.fori_loop(0, sequences, feed, 0)
    mid_back = scatter(part_b, got_b)
    for copy in copies:
        copy.wait_send()

    def leave(b, carry):
        split(plain(hid[b], matrix("d")), part_a, b)
        return carry

    lax.fori_loop(0, sequences, leave, 0)
    out_back = scatter(part_a, got_c)

    def flat(ref):
        return ref.reshape(sequences * length, ref.shape[-1])

    def weigh(name, left, right):
        _, _, off, size = plan[name]
        right = right[...].reshape(sequences * length, width)
        chunk = 256

        def some(i, carry):
            at = pl.multiple_of(i * chunk, chunk)
            lhs = left[:, :, pl.ds(at, chunk)].reshape(sequences * length, chunk)
            gb[rows(off + at, chunk, 64), :] = over_tokens(lhs, right).astype(jnp.bfloat16)
            return carry

        lax.fori_loop(0, 4 * size // chunk, some, 0)
        return send(
            gb.at[rows(off + (1 - core) * 2 * size, 2 * size, 64)],
            rk.at[pl.ds(off // 2, 2 * size)],
            shard=sib,
        )

    def drain_core(name, copy):
        _, _, off, size = plan[name]
        arrive([copy])
        here = rows(off + theirs * size, size, 64)
        there = rows(off // 2 + (1 - side) * size, size, 64)
        total = gb[here, :].astype(jnp.float32) + rk[there, :].astype(jnp.float32)
        at = pl.ds(off // 4, size)
        hs[at, :] = total.astype(jnp.bfloat16)
        return send(hs.at[at], ry.at[at], shard=opp)

    def drain_side(name, copy):
        own, own_size, off, size = plan[name]
        arrive([copy])
        here = rows(off + mine * size, size, 64)
        there = rows(off // 2 + side * size, size, 64)
        total = gb[here, :].astype(jnp.float32) + rk[there, :].astype(jnp.float32)
        total = total + ry[pl.ds(off // 4, size), :].astype(jnp.float32)
        total = total.astype(jnp.bfloat16)
        at = pl.ds(own, own_size)
        if own_size == size:
            xo[at, :] = total
            return send(xo.at[at], rx.at[at], rep=1 - r)
        i = "kv".index(name)
        kvh[i] = total
        return send(kvh.at[i, rows((1 - half) * own_size, own_size, 64)], kvr.at[i], ctx=partner)

    def drain_pair(name, copy):
        own, own_size, _, _ = plan[name]
        arrive([copy])
        i = "kv".index(name)
        total = kvh[i, rows(half * own_size, own_size, 64), :].astype(jnp.float32)
        at = pl.ds(own, own_size)
        xo[at, :] = (total + kvr[i].astype(jnp.float32)).astype(jnp.bfloat16)
        return send(xo.at[at], rx.at[at], rep=1 - r)

    def drain_rep(name, copy):
        at = own_rows(name)
        arrive([copy])
        grad_w[at, :] = xo[at, :].astype(jnp.float32) + rx[at, :].astype(jnp.float32)

    moving = {}
    moving["d"] = weigh("d", hid, c_all)
    moving["g"] = weigh("g", dga, nm)
    moving["u"] = weigh("u", dup, nm)

    dgt[...] = jnp.zeros_like(dgt)
    arrive(mid_back)
    for b in range(sequences):
        d_mid = collect(part_b, got_b, b)
        m = mixed[b]
        r_mid = rms_scale(m)
        dgt[1:2, :] += jnp.sum(d_mid * m * r_mid, axis=0, keepdims=True)
        d_resid = cot[b].astype(jnp.float32) + norm_backward(d_mid, m, r_mid, g_mlp)
        dres[b] = d_resid
        own_res[b] = d_resid.astype(jnp.bfloat16)
    res_in = gather(own_res, res)
    keep(own_res, res)
    for n in "dgu":
        moving[n] = drain_core(n, moving[n])
    arrive(out_back)
    for b in range(sequences):
        block_out[b] = (mixed[b] + collect(part_a, got_c, b)).astype(jnp.bfloat16)
    for copy in mid_back:
        copy.wait_send()
    arrive(res_in)
    moving["o"] = weigh("o", att, res)

    def attend_back(b, carry):
        d_att = against_rows(whole(res, b), matrix("o")).astype(jnp.bfloat16)
        cos_b, sin_b = cosine[b], sine[b]

        def through(d_rot, u, gain):
            d_n = d_rot * cos_b - swap_halves(d_rot) * sin_b
            u_scale = rms_scale(u)
            gain_row = jnp.sum(d_n * u * u_scale, axis=0, keepdims=True)
            return norm_backward(d_n, u, u_scale, gain).astype(jnp.bfloat16), gain_row

        for h in range(heads):
            at = slice(h * HEAD_DIM, (h + 1) * HEAD_DIM)
            da, p = d_att[:, at], prob[b, h]
            delta = jnp.sum(
                da.astype(jnp.float32) * att[b, :, at].astype(jnp.float32), axis=-1, keepdims=True
            )
            dvb[b, :, at] = over_tokens(p.astype(jnp.bfloat16), da).astype(jnp.bfloat16)
            d_p = against_rows(da, vb[b, h])
            d_s = (p * (d_p - delta)).astype(jnp.bfloat16)
            d_q, row_q = through(plain(d_s, kr[b, h]) * scale, qf[b, h], g_query)
            d_k, row_k = through(over_tokens(d_s, qr[b, h]) * scale, kf[b, h], g_key)
            dqb[b, :, at] = d_q
            dkb[b, :, at] = d_k
            dgt[2:3, :HEAD_DIM] += row_q
            dgt[2:3, HEAD_DIM : 2 * HEAD_DIM] += row_k
        d_in = plain(dqb[b], matrix("q")) + plain(dkb[b], matrix("k")) + plain(dvb[b], matrix("v"))
        split(d_in, part_b, b)
        return carry

    lax.fori_loop(0, sequences, attend_back, 0)
    in_back = scatter(part_b, got_d)
    moving["q"] = weigh("q", dqb, nx)
    moving["k"] = weigh("k", dkb, nx)
    moving["v"] = weigh("v", dvb, nx)
    for n in "dgu":
        moving[n] = drain_side(n, moving[n])
    for n in "okvq":
        moving[n] = drain_core(n, moving[n])
    arrive(in_back)
    for b in range(sequences):
        d_in = collect(part_b, got_d, b)
        x = tok[b].astype(jnp.float32)
        r_in = rms_scale(x)
        dgt[0:1, :] += jnp.sum(d_in * x * r_in, axis=0, keepdims=True)
        grad_in[b] = dres[b] + norm_backward(d_in, x, r_in, g_attn)
    gains = [send(dgt, dz.at[d - 1], ctx=around(d)) for d in steps]
    for n in "okv":
        moving[n] = drain_side(n, moving[n])
    arrive(gains)
    total = dgt[...]
    for d in steps:
        total = total + dz[d - 1]
    dsum[...] = total
    gains = [send(dsum, dz_s.at[i], shard=p) for i, p in enumerate((sib, opp, dia))]
    moving["q"] = drain_side("q", moving["q"])
    for n in "dgu":
        drain_rep(n, moving[n])
    arrive(gains)
    dtot[...] = dsum[...] + dz_s[0] + dz_s[1] + dz_s[2]
    gains = [send(dtot, dz_x, rep=1 - r)]
    for n in "kv":
        moving[n] = drain_pair(n, moving[n])
    for n in "oqkv":
        drain_rep(n, moving[n])
    arrive(gains)
    gain_out[...] = dtot[...] + dz_x[...]
    waited = {id(copy) for copy in copies + mid_back}
    for copy in sends:
        if id(copy) not in waited:
            copy.wait_send()


def whole_layer_body(
    tokens,
    positions,
    segments,
    cotangent,
    w_query,
    key_weight,
    value_weight,
    output_weight,
    w_gate,
    w_up,
    w_down,
    norm_gains,
):
    sequences, span, width = tokens.shape
    ctx = lax.axis_size("ctx")
    length = span * ctx
    ff = w_gate.shape[1]
    half = key_weight.shape[1]
    plan, own_total, full_total = row_plan(half, ff)
    heads = 4
    stacked = jnp.concatenate(
        [
            w_query.T,
            key_weight.T,
            value_weight.T,
            output_weight,
            w_gate.T,
            w_up.T,
            w_down,
        ],
        axis=0,
    )
    count = norm_gains.shape[0]
    place = lax.axis_index("shard") * ctx + lax.axis_index("ctx")
    all_gains = width * 2 + 2 * HEAD_DIM
    spread_gains = lax.dynamic_update_slice(
        jnp.zeros((all_gains,), jnp.float32), norm_gains.astype(jnp.float32), (place * count,)
    )
    gain_rows = jnp.concatenate(
        [
            spread_gains[:width],
            spread_gains[width + 2 * HEAD_DIM :],
            spread_gains[width : width + 2 * HEAD_DIM],
            jnp.zeros((6 * width - 2 * HEAD_DIM,), jnp.float32),
        ]
    ).reshape(8, width)
    cosine, sine = rope_tables(positions)
    cosine, sine = cosine[:, :, 0], sine[:, :, 0]
    cosine = jnp.concatenate([cosine, cosine], axis=-1)
    sine = jnp.concatenate([-sine, sine], axis=-1)
    allowed = (
        (segments[:, :, None] == segments[:, None, :])
        & (positions[:, None, :] <= positions[:, :, None])
    ).astype(jnp.float32)

    bf, f32 = jnp.bfloat16, jnp.float32
    gathered = pltpu.VMEM((sequences, ctx, span, width), bf)
    own_block = pltpu.VMEM((sequences, span, width), bf)
    own_float = pltpu.VMEM((sequences, span, width), f32)
    head_float = pltpu.VMEM((sequences, heads, length, HEAD_DIM), f32)
    head_half = pltpu.VMEM((sequences, heads, length, HEAD_DIM), bf)
    head_lanes = pltpu.VMEM((sequences, length, heads * HEAD_DIM), bf)
    ff_lanes = pltpu.VMEM((sequences, length, heads * ff), bf)
    parts = pltpu.VMEM((ctx, sequences, span, width), bf)
    got = pltpu.VMEM((ctx - 1, sequences, span, width), bf)
    tile = pltpu.VMEM((8, width), f32)
    tiles_c = pltpu.VMEM((ctx - 1, 8, width), f32)
    tiles_s = pltpu.VMEM((3, 8, width), f32)

    def row_buffer(n):
        return pltpu.VMEM((n, width), bf)

    copies = 128
    vmem = pl.BlockSpec(memory_space=pltpu.VMEM)
    block_out, grad_input, grads, gains_sum = pl.pallas_call(
        functools.partial(layer_kernel, plan),
        out_shape=(
            jax.ShapeDtypeStruct(tokens.shape, bf),
            jax.ShapeDtypeStruct(tokens.shape, f32),
            jax.ShapeDtypeStruct((own_total, width), f32),
            jax.ShapeDtypeStruct((8, width), f32),
        ),
        in_specs=[vmem] * 7,
        out_specs=[vmem] * 4,
        scratch_shapes=[
            gathered,
            gathered,
            gathered,
            gathered,
            gathered,
            own_block,
            own_block,
            row_buffer(full_total),
            head_float,
            head_float,
            head_half,
            head_half,
            head_half,
            pltpu.VMEM((sequences, heads, length, length), f32),
            head_lanes,
            ff_lanes,
            ff_lanes,
            ff_lanes,
            head_lanes,
            head_lanes,
            head_lanes,
            own_float,
            own_float,
            parts,
            parts,
            got,
            got,
            got,
            got,
            tiles_c,
            tile,
            tiles_s,
            tile,
            tile,
            tiles_c,
            tile,
            tiles_s,
            tile,
            tile,
            row_buffer(full_total),
            row_buffer(full_total // 2),
            row_buffer(full_total // 4),
            row_buffer(full_total // 4),
            pltpu.VMEM((2, HEAD_DIM, width), bf),
            pltpu.VMEM((2, half, width), bf),
            row_buffer(own_total),
            row_buffer(own_total),
            pltpu.SemaphoreType.DMA((copies,)),
            pltpu.SemaphoreType.DMA((copies,)),
        ],
        compiler_params=pltpu.CompilerParams(
            collective_id=0, has_side_effects=True, vmem_limit_bytes=67043328
        ),
    )(tokens, cotangent, stacked, gain_rows, allowed, cosine, sine)

    def part(name):
        at, size = plan[name][:2]
        return grads[at : at + size]

    flat = jnp.concatenate([gains_sum[0], gains_sum[2, : 2 * HEAD_DIM], gains_sum[1]])
    return (
        block_out,
        grad_input,
        part("q").T,
        part("k").T,
        part("v").T,
        part("o"),
        part("g").T,
        part("u").T,
        part("d"),
        lax.dynamic_slice(flat, (place * count,), (count,)),
    )


def any_body(*arguments):
    tokens, w_query, key_weight, w_gate = (arguments[i] for i in (0, 4, 5, 8))
    ctx, shards = lax.axis_size("ctx"), lax.axis_size("shard")
    fits = w_query.shape[1] == HEAD_DIM and 2 * key_weight.shape[1] == HEAD_DIM
    fits = fits and lax.axis_size("rep") == 2 and shards == 4 and ctx % 2 == 0
    fits = fits and w_gate.shape[1] % 64 == 0 and tokens.shape[1] % 16 == 0
    fits = fits and tokens.shape[0] * tokens.shape[1] * ctx <= 512
    if fits:
        return whole_layer_body(*arguments)
    return body(*arguments)


def solution(mesh):
    in_specs = (
        P(("rep", "shard"), "ctx", None),
        P(("rep", "shard"), None),
        P(("rep", "shard"), None),
        P(("rep", "shard"), "ctx", None),
        P(None, ("shard", "ctx")),
        P(None, ("shard", "ctx")),
        P(None, ("shard", "ctx")),
        P(("shard", "ctx"), None),
        P(None, ("shard", "ctx")),
        P(None, ("shard", "ctx")),
        P(("shard", "ctx"), None),
        P(("shard", "ctx")),
    )
    out_specs = (
        P(("rep", "shard"), "ctx", None),
        P(("rep", "shard"), "ctx", None),
        P(None, ("shard", "ctx")),
        P(None, ("shard", "ctx")),
        P(None, ("shard", "ctx")),
        P(("shard", "ctx"), None),
        P(None, ("shard", "ctx")),
        P(None, ("shard", "ctx")),
        P(("shard", "ctx"), None),
        P(("shard", "ctx")),
    )
    return jax.shard_map(any_body, mesh=mesh, in_specs=in_specs, out_specs=out_specs, check_vma=False)
```

```python
import functools
import math

import jax
import jax.numpy as jnp
from jax import lax
from jax.experimental import pallas as pl
from jax.experimental.pallas import tpu as pltpu
from jax.sharding import PartitionSpec as P

QUERY_HEADS = 16
KEY_VALUE_HEADS = 8
HEAD_DIM = 128

MESH = pl.DeviceIdType.MESH

EPSILON = 1e-06
ROPE_BASE = 1000000.0


def rms_scale(values_in):
    return lax.rsqrt(jnp.mean(values_in * values_in, axis=-1, keepdims=True) + EPSILON)


def norm_backward(grad_in, values_in, scale_in, gain_in):
    grad_norm = grad_in * gain_in
    unit = values_in * scale_in
    return scale_in * (grad_norm - unit * jnp.mean(grad_norm * unit, axis=-1, keepdims=True))


def rope_tables(position_ids):
    half_dim = HEAD_DIM // 2
    inverse = 1.0 / ROPE_BASE ** (jnp.arange(half_dim, dtype=jnp.float32) * (2.0 / HEAD_DIM))
    angle = position_ids.astype(jnp.float32)[..., None] * inverse
    return (jnp.cos(angle)[:, :, None, :], jnp.sin(angle)[:, :, None, :])


def rotate(values_in, cosine, sine):
    half_dim = values_in.shape[-1] // 2
    first = values_in[..., :half_dim]
    second = values_in[..., half_dim:]
    return jnp.concatenate(
        [first * cosine - second * sine, second * cosine + first * sine], axis=-1
    )


def rotate_back(grad_in, cosine, sine):
    half_dim = grad_in.shape[-1] // 2
    first = grad_in[..., :half_dim]
    second = grad_in[..., half_dim:]
    return jnp.concatenate(
        [first * cosine + second * sine, second * cosine - first * sine], axis=-1
    )


def float_product(left, right):
    return jnp.dot(left, right, preferred_element_type=jnp.float32)


def against_rows(left, right):
    return lax.dot_general(
        left, right, (((1,), (1,)), ((), ())), preferred_element_type=jnp.float32
    )


def over_tokens(left, right):
    return lax.dot_general(
        left, right, (((0,), (0,)), ((), ())), preferred_element_type=jnp.float32
    )


def body(
    tokens,
    positions,
    segments,
    cotangent,
    w_query,
    key_weight,
    value_weight,
    output_weight,
    w_gate,
    w_up,
    w_down,
    norm_gains,
):
    sequence_count, local_length, model_width = tokens.shape
    total_rows = sequence_count * local_length
    group_width = QUERY_HEADS // KEY_VALUE_HEADS
    score_scale = 1.0 / math.sqrt(HEAD_DIM)
    local_start = lax.axis_index("ctx") * local_length
    local_pos = lax.dynamic_slice_in_dim(positions, local_start, local_length, 1)
    local_seg = lax.dynamic_slice_in_dim(segments, local_start, local_length, 1)
    wq_full, full_key_weight, full_value_weight, wo_full, gains_full = (
        lax.all_gather(w_query, ("shard", "ctx"), axis=1, tiled=True),
        lax.all_gather(key_weight, ("shard", "ctx"), axis=1, tiled=True),
        lax.all_gather(value_weight, ("shard", "ctx"), axis=1, tiled=True),
        lax.all_gather(output_weight, ("shard", "ctx"), axis=0, tiled=True),
        lax.all_gather(norm_gains, ("shard", "ctx"), axis=0, tiled=True),
    )
    gain_all = gains_full.astype(jnp.float32)
    g_attn = gain_all[:model_width]
    g_query = gain_all[model_width : model_width + HEAD_DIM]
    key_gain = gain_all[model_width + HEAD_DIM : model_width + 2 * HEAD_DIM]
    g_mlp = gain_all[model_width + 2 * HEAD_DIM :]
    x_rows = tokens.reshape(total_rows, model_width).astype(jnp.float32)
    scale_in = rms_scale(x_rows)
    normed_input = (x_rows * scale_in * g_attn).astype(jnp.bfloat16)
    query = float_product(normed_input, wq_full).reshape(
        sequence_count, local_length, QUERY_HEADS, HEAD_DIM
    )
    key_rows = float_product(normed_input, full_key_weight).reshape(
        sequence_count, local_length, KEY_VALUE_HEADS, HEAD_DIM
    )
    value_rows = (
        float_product(normed_input, full_value_weight)
        .astype(jnp.bfloat16)
        .reshape(sequence_count, local_length, KEY_VALUE_HEADS, HEAD_DIM)
    )
    q_scale = rms_scale(query)
    key_scale = rms_scale(key_rows)
    cosine, sine = rope_tables(local_pos)
    query_rotated = rotate(query * q_scale * g_query, cosine, sine).astype(jnp.bfloat16)
    k_rot = rotate(key_rows * key_scale * key_gain, cosine, sine).astype(jnp.bfloat16)
    keys_all, values_all = (
        lax.all_gather(k_rot, "ctx", axis=1, tiled=True),
        lax.all_gather(value_rows, "ctx", axis=1, tiled=True),
    )
    allowed = (
        (local_seg[:, :, None] == segments[:, None, :])
        & (positions[:, None, :] <= local_pos[:, :, None])
    )[:, None, None]
    query_group = query_rotated.reshape(
        sequence_count, local_length, KEY_VALUE_HEADS, group_width, HEAD_DIM
    )
    scores = (
        jnp.einsum("bqkgd,bskd->bkgqs", query_group, keys_all, preferred_element_type=jnp.float32)
        * score_scale
    )
    exponent = jnp.where(allowed, jnp.exp(scores), 0.0)
    denominator = jnp.sum(exponent, axis=-1)
    log_total = jnp.log(denominator)
    probs = (exponent / denominator[..., None]).astype(jnp.bfloat16)
    attention_output = jnp.einsum(
        "bkgqs,bskd->bqkgd", probs, values_all, preferred_element_type=jnp.float32
    )
    attention_output = attention_output.astype(jnp.bfloat16).reshape(
        total_rows, QUERY_HEADS * HEAD_DIM
    )
    mixed_in = x_rows + float_product(attention_output, wo_full)
    scale_mid = rms_scale(mixed_in)
    normed_mid = (mixed_in * scale_mid * g_mlp).astype(jnp.bfloat16)
    wg_full, wu_full, wd_full = (
        lax.all_gather(w_gate, ("shard", "ctx"), axis=1, tiled=True),
        lax.all_gather(w_up, ("shard", "ctx"), axis=1, tiled=True),
        lax.all_gather(w_down, ("shard", "ctx"), axis=0, tiled=True),
    )
    gate_pre = float_product(normed_mid, wg_full)
    up_pre = float_product(normed_mid, wu_full)
    sigmoid_gate = jax.nn.sigmoid(gate_pre)
    hidden = (gate_pre * sigmoid_gate * up_pre).astype(jnp.bfloat16)
    block_sum = mixed_in + float_product(hidden, wd_full)
    block_out = block_sum.astype(jnp.bfloat16).reshape(sequence_count, local_length, model_width)
    grad_rows = cotangent.reshape(total_rows, model_width)
    d_hidden = against_rows(grad_rows, wd_full)
    grad_down = over_tokens(hidden, grad_rows)
    d_gate = (d_hidden * up_pre * sigmoid_gate * (1.0 + gate_pre * (1.0 - sigmoid_gate))).astype(
        jnp.bfloat16
    )
    d_up = (d_hidden * gate_pre * sigmoid_gate).astype(jnp.bfloat16)
    grad_gate = over_tokens(normed_mid, d_gate)
    grad_up = over_tokens(normed_mid, d_up)
    owned_gate, owned_up, owned_down = (
        lax.psum_scatter(grad_gate, ("shard", "ctx"), scatter_dimension=1, tiled=True),
        lax.psum_scatter(grad_up, ("shard", "ctx"), scatter_dimension=1, tiled=True),
        lax.psum_scatter(grad_down, ("shard", "ctx"), scatter_dimension=0, tiled=True),
    )
    total_gate, total_up, total_down = (
        lax.psum(owned_gate.astype(jnp.bfloat16), "rep").astype(jnp.float32),
        lax.psum(owned_up.astype(jnp.bfloat16), "rep").astype(jnp.float32),
        lax.psum(owned_down.astype(jnp.bfloat16), "rep").astype(jnp.float32),
    )
    d_mid = against_rows(d_gate, wg_full) + against_rows(d_up, wu_full)
    dg_mlp = jnp.sum(d_mid * mixed_in * scale_mid, axis=0)
    d_resid = grad_rows.astype(jnp.float32) + norm_backward(d_mid, mixed_in, scale_mid, g_mlp)
    residual_gradient_bfloat = d_resid.astype(jnp.bfloat16)
    grad_output = over_tokens(attention_output, residual_gradient_bfloat)
    attention_gradient = (
        against_rows(residual_gradient_bfloat, wo_full)
        .astype(jnp.bfloat16)
        .reshape(sequence_count, local_length, KEY_VALUE_HEADS, group_width, HEAD_DIM)
    )
    attention_heads = attention_output.reshape(
        sequence_count, local_length, KEY_VALUE_HEADS, group_width, HEAD_DIM
    )
    row_delta = jnp.sum(
        attention_gradient.astype(jnp.float32) * attention_heads.astype(jnp.float32), axis=-1
    )
    row_delta = jnp.transpose(row_delta, (0, 2, 3, 1))
    scores_again = (
        jnp.einsum("bqkgd,bskd->bkgqs", query_group, keys_all, preferred_element_type=jnp.float32)
        * score_scale
    )
    probs_back = jnp.where(allowed, jnp.exp(scores_again - log_total[..., None]), 0.0)
    probs_round = probs_back.astype(jnp.bfloat16)
    values_gradient = jnp.einsum(
        "bkgqs,bqkgd->bskd", probs_round, attention_gradient, preferred_element_type=jnp.float32
    )
    d_probs = jnp.einsum(
        "bqkgd,bskd->bkgqs", attention_gradient, values_all, preferred_element_type=jnp.float32
    )
    d_scores = (probs_back * (d_probs - row_delta[..., None])).astype(jnp.bfloat16)
    d_qrot = (
        jnp.einsum("bkgqs,bskd->bqkgd", d_scores, keys_all, preferred_element_type=jnp.float32)
        * score_scale
    )
    d_krot = (
        jnp.einsum("bkgqs,bqkgd->bskd", d_scores, query_group, preferred_element_type=jnp.float32)
        * score_scale
    )
    d_keys, value_rows_gradient = (
        lax.psum_scatter(
            d_krot.astype(jnp.bfloat16), "ctx", scatter_dimension=1, tiled=True
        ).astype(jnp.float32),
        lax.psum_scatter(
            values_gradient.astype(jnp.bfloat16), "ctx", scatter_dimension=1, tiled=True
        ).astype(jnp.float32),
    )
    d_qn = rotate_back(
        d_qrot.reshape(sequence_count, local_length, QUERY_HEADS, HEAD_DIM), cosine, sine
    )
    normed_key_gradient = rotate_back(d_keys, cosine, sine)
    dg_query = jnp.sum(d_qn * query * q_scale, axis=(0, 1, 2))
    dg_key = jnp.sum(normed_key_gradient * key_rows * key_scale, axis=(0, 1, 2))
    d_query = (
        norm_backward(d_qn, query, q_scale, g_query)
        .astype(jnp.bfloat16)
        .reshape(total_rows, QUERY_HEADS * HEAD_DIM)
    )
    key_gradient = (
        norm_backward(normed_key_gradient, key_rows, key_scale, key_gain)
        .astype(jnp.bfloat16)
        .reshape(total_rows, KEY_VALUE_HEADS * HEAD_DIM)
    )
    value_gradient = value_rows_gradient.astype(jnp.bfloat16).reshape(
        total_rows, KEY_VALUE_HEADS * HEAD_DIM
    )
    grad_query = over_tokens(normed_input, d_query)
    grad_key = over_tokens(normed_input, key_gradient)
    grad_value = over_tokens(normed_input, value_gradient)
    d_in = (
        against_rows(d_query, wq_full)
        + against_rows(key_gradient, full_key_weight)
        + against_rows(value_gradient, full_value_weight)
    )
    dg_attn = jnp.sum(d_in * x_rows * scale_in, axis=0)
    grad_input = (d_resid + norm_backward(d_in, x_rows, scale_in, g_attn)).reshape(
        sequence_count, local_length, model_width
    )
    grad_gains = jnp.concatenate([dg_attn, dg_query, dg_key, dg_mlp])
    owned_query, owned_key, owned_value, owned_output, owned_gains = (
        lax.psum_scatter(grad_query, ("shard", "ctx"), scatter_dimension=1, tiled=True),
        lax.psum_scatter(grad_key, ("shard", "ctx"), scatter_dimension=1, tiled=True),
        lax.psum_scatter(grad_value, ("shard", "ctx"), scatter_dimension=1, tiled=True),
        lax.psum_scatter(grad_output, ("shard", "ctx"), scatter_dimension=0, tiled=True),
        lax.psum_scatter(grad_gains, ("shard", "ctx"), scatter_dimension=0, tiled=True),
    )
    total_query, total_key, total_value, total_output, total_gains = (
        lax.psum(owned_query.astype(jnp.bfloat16), "rep").astype(jnp.float32),
        lax.psum(owned_key.astype(jnp.bfloat16), "rep").astype(jnp.float32),
        lax.psum(owned_value.astype(jnp.bfloat16), "rep").astype(jnp.float32),
        lax.psum(owned_output.astype(jnp.bfloat16), "rep").astype(jnp.float32),
        lax.psum(owned_gains.astype(jnp.bfloat16), "rep").astype(jnp.float32),
    )
    return (
        block_out,
        grad_input,
        total_query,
        total_key,
        total_value,
        total_output,
        total_gate,
        total_up,
        total_down,
        total_gains,
    )


def row_plan(head_half, ff):
    sizes = (
        ("q", HEAD_DIM, HEAD_DIM),
        ("k", head_half, HEAD_DIM),
        ("v", head_half, HEAD_DIM),
        ("o", HEAD_DIM, HEAD_DIM),
        ("g", ff, ff),
        ("u", ff, ff),
        ("d", ff, ff),
    )
    plan, own, full = {}, 0, 0
    for name, own_rows, block_rows in sizes:
        plan[name] = (own, own_rows, full, block_rows)
        own, full = own + own_rows, full + 4 * block_rows
    return plan, own, full


def plain(left, right):
    return lax.dot_general(left, right, (((1,), (0,)), ((), ())), preferred_element_type=jnp.float32)


def swap_halves(values_in):
    return pltpu.roll(values_in, values_in.shape[-1] // 2, 1)


def rows(start, size, step):
    return pl.ds(pl.multiple_of(start, step), size)


def layer_kernel(
    plan,
    tok,
    cot,
    columns,
    out_rows,
    down_rows,
    gain_in,
    pos,
    seg,
    cosine,
    sine,
    block_out,
    grad_in,
    grad_q,
    grad_k,
    grad_v,
    grad_o,
    grad_g,
    grad_u,
    grad_d,
    gain_out,
    x_all,
    c_all,
    nx,
    nm,
    res,
    own_mid,
    own_res,
    turned,
    wb,
    qf,
    kf,
    qr,
    kr,
    vb,
    prob,
    att,
    hid,
    dga,
    dup,
    dqb,
    dkb,
    dvb,
    mixed,
    dres,
    part_a,
    part_b,
    got_a,
    got_b,
    got_c,
    got_d,
    gz,
    gsum,
    gz_s,
    gfull,
    dgt,
    dz,
    dsum,
    dz_s,
    dtot,
    dz_x,
    gb,
    rk,
    hs,
    ry,
    kvh,
    kvr,
    xo,
    rx,
    send_sem,
    recv_sem,
):
    sequences, span, width = tok.shape
    ctx = lax.axis_size("ctx")
    length = span * ctx
    heads = 4
    scale = 1.0 / math.sqrt(HEAD_DIM)
    r, s, c = lax.axis_index("rep"), lax.axis_index("shard"), lax.axis_index("ctx")
    core, side = s % 2, s // 2
    sib, opp = s + 1 - 2 * core, (s + 2) % 4
    dia = (sib + 2) % 4
    mine, theirs = core * 2 + side, core * 2 + 1 - side
    half = c % 2
    near = c + 1 - 2 * half
    far = (c + 2) % 4
    other = (near + 2) % 4
    both = range(sequences)
    sends, lent, returned = [], [], []

    def send(src, dst, **where):
        at = len(sends)
        copy = pltpu.make_async_remote_copy(
            src_ref=src,
            dst_ref=dst,
            send_sem=send_sem.at[at],
            recv_sem=recv_sem.at[at],
            device_id=where,
            device_id_type=MESH,
        )
        copy.start()
        sends.append(copy)
        return copy

    def arrive(copies):
        for copy in copies:
            copy.wait_recv()

    def reclaim(copies):
        for copy in copies:
            copy.wait_send()
            returned.append(copy)

    def gather_start(src, dst, b):
        dst[b, c] = src[b]
        across = send(src.at[b], dst.at[b, c], ctx=far)
        beside = send(src.at[b], dst.at[b, c], ctx=near)
        return beside, across

    def gather_pass(dst, b, pair):
        arrive([pair[1]])
        return pair[0], send(dst.at[b, far], dst.at[b, far], ctx=near)

    def reduce_start(src, got, b):
        first = send(src.at[other, b], got.at[0, b], ctx=near)
        second = send(src.at[near, b], got.at[1, b], ctx=near)
        lent.extend((first, second))
        return first, second

    def reduce_pass(src, got, b, pair):
        arrive([pair[0]])
        total = src[far, b].astype(jnp.float32) + got[0, b].astype(jnp.float32)
        src[far, b] = total.astype(jnp.bfloat16)
        third = send(src.at[far, b], got.at[2, b], ctx=far)
        lent.append(third)
        return pair[1], third

    def reduce_end(src, got, b, pair):
        arrive(pair)
        total = src[c, b].astype(jnp.float32) + got[1, b].astype(jnp.float32)
        return total + got[2, b].astype(jnp.float32)

    def block(name, at):
        _, _, off, size = plan[name]
        return rows(off + at * size, size, 64)

    def spread_rows(own):
        there = send(wb.at[own], wb.at[own], shard=opp)
        return [there], [send(wb.at[own], wb.at[own], shard=sib)]

    def spread(name):
        return spread_rows(block(name, mine))

    def pass_on(name):
        got = block(name, theirs)
        return send(wb.at[got], wb.at[got], shard=sib)

    def own_rows(name):
        off, size = plan[name][:2]
        return pl.ds(off, size)

    def matrix(name):
        _, _, off, size = plan[name]
        return wb[pl.ds(off, 4 * size), :]

    def whole(ref, b):
        return ref[b].reshape(length, width)

    def split(values_in, dst, b):
        for j in range(ctx):
            dst[j, b] = values_in[j * span : (j + 1) * span].astype(jnp.bfloat16)

    def turn(first):
        at = pl.ds(first, HEAD_DIM)
        turned[at, :] = columns[:, at].astype(jnp.float32).T.astype(jnp.bfloat16)

    barrier = pltpu.get_barrier_semaphore()
    peers = [{"ctx": near}, {"ctx": far}, {"ctx": other}]
    peers += [{"shard": sib}, {"shard": opp}, {"shard": dia}, {"rep": 1 - r}]
    for peer in peers:
        pl.semaphore_signal(barrier, inc=1, device_id=peer, device_id_type=MESH)
    pl.semaphore_wait(barrier, len(peers))

    head_half, ff = plan["k"][1], plan["g"][1]
    turn(HEAD_DIM)
    kv_in, spreads = [], {}
    for i, n in enumerate("kv"):
        first = plan[n][2] + mine * HEAD_DIM
        at = rows(first + half * head_half, head_half, 64)
        wb[at, :] = turned[pl.ds(HEAD_DIM + i * head_half, head_half), :]
        kv_in.append(send(wb.at[at], wb.at[at], ctx=near))
        spreads[n] = spread_rows(at)
    tok_in = [gather_start(tok, x_all, b) for b in both]
    gains = [send(gain_in, gz.at[i], ctx=p) for i, p in enumerate((near, far, other))]
    turn(0)
    wb[block("q", mine), :] = turned[pl.ds(0, HEAD_DIM), :]
    spreads["q"] = spread("q")
    wb[block("o", mine), :] = out_rows[...]
    arrive(kv_in)
    for n in "kv":
        first = plan[n][2] + mine * HEAD_DIM
        late = spread_rows(rows(first + (1 - half) * head_half, head_half, 64))
        for early, more in zip(spreads[n], late):
            early.extend(more)
    spreads["o"] = spread("o")
    arrive(gains)
    gsum[...] = gain_in[...] + gz[0] + gz[1] + gz[2]
    gains = [send(gsum, gz_s.at[i], shard=p) for i, p in enumerate((sib, opp, dia))]
    for first in range(2 * HEAD_DIM, turned.shape[0], HEAD_DIM):
        turn(first)
    wb[block("g", mine), :] = turned[pl.ds(2 * HEAD_DIM, ff), :]
    wb[block("u", mine), :] = turned[pl.ds(2 * HEAD_DIM + ff, ff), :]
    wb[block("d", mine), :] = down_rows[...]
    tok_in = [gather_pass(x_all, b, tok_in[b]) for b in both]
    arrive(gains)
    gfull[...] = gsum[...] + gz_s[0] + gz_s[1] + gz_s[2]
    g_attn = gfull[0:1, :]
    g_mlp = gfull[1:2, :]
    g_query = gfull[2:3, :HEAD_DIM]
    g_key = gfull[2:3, HEAD_DIM : 2 * HEAD_DIM]
    passed = {}

    def pass_weights(names):
        for n in names:
            arrive(spreads[n][0])
            passed[n] = pass_on(n)

    def have_weights(names):
        for n in names:
            arrive(spreads[n][1] + [passed[n]])

    pass_weights("qkv")

    def norm_rows(b):
        def one(j, carry):
            x = x_all[b, j].astype(jnp.float32)
            nx[b, j] = (x * rms_scale(x) * g_attn).astype(jnp.bfloat16)
            return carry

        lax.fori_loop(0, ctx, one, 0)

    def attend(b):
        x = whole(nx, b)
        query = against_rows(x, matrix("q"))
        key = against_rows(x, matrix("k"))
        value = against_rows(x, matrix("v")).astype(jnp.bfloat16)
        cos_b, sin_b = cosine[b], sine[b]
        key_at = jnp.broadcast_to(pos[b : b + 1, :].astype(jnp.float32), (length, length))
        key_doc = jnp.broadcast_to(seg[b : b + 1, :].astype(jnp.float32), (length, length))
        allowed = (key_doc.T == key_doc) & (key_at <= key_at.T)
        for h in range(heads):
            at = slice(h * HEAD_DIM, (h + 1) * HEAD_DIM)
            q, k, v = query[:, at], key[:, at], value[:, at]
            qn = q * rms_scale(q) * g_query
            kn = k * rms_scale(k) * g_key
            q_rot = (qn * cos_b + swap_halves(qn) * sin_b).astype(jnp.bfloat16)
            k_rot = (kn * cos_b + swap_halves(kn) * sin_b).astype(jnp.bfloat16)
            qf[b, h], kf[b, h] = q, k
            qr[b, h], kr[b, h], vb[b, h] = q_rot, k_rot, v
            scores = against_rows(q_rot, k_rot) * scale
            exponent = jnp.where(allowed, jnp.exp(scores), 0.0)
            p = exponent / jnp.sum(exponent, axis=-1, keepdims=True)
            prob[b, h] = p
            att[b, :, at] = plain(p.astype(jnp.bfloat16), v).astype(jnp.bfloat16)

    out_part, cot_in = [], []
    for b in both:
        arrive(tok_in[b])
        norm_rows(b)
        if b == 0:
            have_weights("qkv")
        else:
            cot_in = [gather_start(cot, c_all, i) for i in both]
            for n in "gud":
                spreads[n] = spread(n)
        attend(b)
        if b == 0:
            pass_weights("o")
            have_weights("o")
        else:
            out_part[0] = reduce_pass(part_a, got_a, 0, out_part[0])
        split(plain(att[b], matrix("o")), part_a, b)
        out_part.append(reduce_start(part_a, got_a, b))
    out_part[1] = reduce_pass(part_a, got_a, 1, out_part[1])
    first_parts = list(lent)
    mid_in = []
    for b in both:
        m = tok[b].astype(jnp.float32) + reduce_end(part_a, got_a, b, out_part[b])
        mixed[b] = m
        own_mid[b] = (m * rms_scale(m) * g_mlp).astype(jnp.bfloat16)
        mid_in.append(gather_start(own_mid, nm, b))
        cot_in[b] = gather_pass(c_all, b, cot_in[b])
    pass_weights("gud")
    mid_in = [gather_pass(nm, b, mid_in[b]) for b in both]
    have_weights("gud")

    def feed(b):
        n, ct = whole(nm, b), whole(c_all, b)
        gate = against_rows(n, matrix("g"))
        up = against_rows(n, matrix("u"))
        d_hidden = against_rows(ct, matrix("d"))
        sig = jax.nn.sigmoid(gate)
        hid[b] = (gate * sig * up).astype(jnp.bfloat16)
        d_gate = (d_hidden * up * sig * (1.0 + gate * (1.0 - sig))).astype(jnp.bfloat16)
        d_up = (d_hidden * gate * sig).astype(jnp.bfloat16)
        dga[b], dup[b] = d_gate, d_up
        split(plain(d_gate, matrix("g")) + plain(d_up, matrix("u")), part_b, b)

    mid_back = []
    for b in both:
        arrive(cot_in[b])
        arrive(mid_in[b])
        feed(b)
        mid_back.append(reduce_start(part_b, got_b, b))

    def weigh(name, left, right):
        _, _, off, size = plan[name]
        right = right[...].reshape(sequences * length, width)
        chunk = 256

        def some(i, carry):
            at = pl.multiple_of(i * chunk, chunk)
            lhs = left[:, :, pl.ds(at, chunk)].reshape(sequences * length, chunk)
            gb[rows(off + at, chunk, 64), :] = over_tokens(lhs, right).astype(jnp.bfloat16)
            return carry

        lax.fori_loop(0, 4 * size // chunk, some, 0)
        return send(
            gb.at[rows(off + (1 - core) * 2 * size, 2 * size, 64)],
            rk.at[pl.ds(off // 2, 2 * size)],
            shard=sib,
        )

    def core_sum(name, at):
        _, _, off, size = plan[name]
        here = gb[rows(off + (core * 2 + at) * size, size, 64), :]
        there = rk[rows(off // 2 + at * size, size, 64), :]
        return here.astype(jnp.float32) + there.astype(jnp.float32)

    def drain_core(name, copy):
        _, _, off, size = plan[name]
        arrive([copy])
        at = pl.ds(off // 4, size)
        hs[at, :] = core_sum(name, 1 - side).astype(jnp.bfloat16)
        return send(hs.at[at], ry.at[at], shard=opp)

    def drain_side(name, copy):
        own, own_size, off, size = plan[name]
        arrive([copy])
        total = core_sum(name, side) + ry[pl.ds(off // 4, size), :].astype(jnp.float32)
        total = total.astype(jnp.bfloat16)
        at = pl.ds(own, own_size)
        if own_size == size:
            xo[at, :] = total
            return send(xo.at[at], rx.at[at], rep=1 - r)
        i = "kv".index(name)
        kvh[i] = total
        return send(kvh.at[i, rows((1 - half) * own_size, own_size, 64)], kvr.at[i], ctx=near)

    def drain_pair(name, copy):
        own, own_size, _, _ = plan[name]
        arrive([copy])
        i = "kv".index(name)
        total = kvh[i, rows(half * own_size, own_size, 64), :].astype(jnp.float32)
        at = pl.ds(own, own_size)
        xo[at, :] = (total + kvr[i].astype(jnp.float32)).astype(jnp.bfloat16)
        return send(xo.at[at], rx.at[at], rep=1 - r)

    results = dict(zip("qkvogud", (grad_q, grad_k, grad_v, grad_o, grad_g, grad_u, grad_d)))

    def drain_rep(name, copy):
        at = own_rows(name)
        arrive([copy])
        total = xo[at, :].astype(jnp.float32) + rx[at, :].astype(jnp.float32)
        out = results[name]
        if name in "od":
            out[...] = total
            return
        size = total.shape[0]
        for first in range(0, size, HEAD_DIM):
            piece = total[first : min(first + HEAD_DIM, size)]
            count = piece.shape[0]
            if count < HEAD_DIM:
                piece = jnp.concatenate([piece] * (HEAD_DIM // count), axis=0)
            out[:, first : first + count] = piece.T[:, :count]

    dgt[...] = jnp.zeros_like(dgt)
    res_in = []

    def enter(b):
        d_mid = reduce_end(part_b, got_b, b, mid_back[b])
        m = mixed[b]
        r_mid = rms_scale(m)
        dgt[1:2, :] += jnp.sum(d_mid * m * r_mid, axis=0, keepdims=True)
        d_resid = cot[b].astype(jnp.float32) + norm_backward(d_mid, m, r_mid, g_mlp)
        dres[b] = d_resid
        own_res[b] = d_resid.astype(jnp.bfloat16)
        res_in.append(gather_start(own_res, res, b))

    reclaim(first_parts)
    moving = {}
    moving["d"] = weigh("d", hid, c_all)
    moving["g"] = weigh("g", dga, nm)
    moving["d"] = drain_core("d", moving["d"])
    mid_back[0] = reduce_pass(part_b, got_b, 0, mid_back[0])
    moving["u"] = weigh("u", dup, nm)
    mid_back[1] = reduce_pass(part_b, got_b, 1, mid_back[1])
    second_parts = lent[len(first_parts) :]
    enter(0)
    moving["g"] = drain_core("g", moving["g"])
    enter(1)
    moving["u"] = drain_core("u", moving["u"])
    for b in both:
        split(plain(hid[b], matrix("d")), part_a, b)
    res_in = [gather_pass(res, b, res_in[b]) for b in both]
    out_back = [reduce_start(part_a, got_c, 0)]
    reclaim(second_parts)

    def attend_back(b):
        d_att = against_rows(whole(res, b), matrix("o")).astype(jnp.bfloat16)
        cos_b, sin_b = cosine[b], sine[b]

        def through(d_rot, u, gain):
            d_n = d_rot * cos_b - swap_halves(d_rot) * sin_b
            u_scale = rms_scale(u)
            gain_row = jnp.sum(d_n * u * u_scale, axis=0, keepdims=True)
            return norm_backward(d_n, u, u_scale, gain).astype(jnp.bfloat16), gain_row

        for h in range(heads):
            at = slice(h * HEAD_DIM, (h + 1) * HEAD_DIM)
            da, p = d_att[:, at], prob[b, h]
            delta = jnp.sum(
                da.astype(jnp.float32) * att[b, :, at].astype(jnp.float32), axis=-1, keepdims=True
            )
            dvb[b, :, at] = over_tokens(p.astype(jnp.bfloat16), da).astype(jnp.bfloat16)
            d_p = against_rows(da, vb[b, h])
            d_s = (p * (d_p - delta)).astype(jnp.bfloat16)
            d_q, row_q = through(plain(d_s, kr[b, h]) * scale, qf[b, h], g_query)
            d_k, row_k = through(over_tokens(d_s, qr[b, h]) * scale, kf[b, h], g_key)
            dqb[b, :, at] = d_q
            dkb[b, :, at] = d_k
            dgt[2:3, :HEAD_DIM] += row_q
            dgt[2:3, HEAD_DIM : 2 * HEAD_DIM] += row_k
        d_in = plain(dqb[b], matrix("q")) + plain(dkb[b], matrix("k")) + plain(dvb[b], matrix("v"))
        split(d_in, part_b, b)

    arrive(res_in[0])
    moving["d"] = drain_side("d", moving["d"])
    attend_back(0)
    in_back = [reduce_start(part_b, got_d, 0)]
    out_back[0] = reduce_pass(part_a, got_c, 0, out_back[0])
    arrive(res_in[1])
    moving["o"] = weigh("o", att, res)
    moving["g"] = drain_side("g", moving["g"])
    moving["o"] = drain_core("o", moving["o"])
    attend_back(1)
    in_back.append(reduce_start(part_b, got_d, 1))
    moving["k"] = weigh("k", dkb, nx)
    in_back[0] = reduce_pass(part_b, got_d, 0, in_back[0])
    moving["v"] = weigh("v", dvb, nx)
    moving["k"] = drain_core("k", moving["k"])
    moving["q"] = weigh("q", dqb, nx)
    moving["v"] = drain_core("v", moving["v"])
    moving["q"] = drain_core("q", moving["q"])
    moving["u"] = drain_side("u", moving["u"])
    in_back[1] = reduce_pass(part_b, got_d, 1, in_back[1])
    out_back.append(reduce_start(part_a, got_c, 1))
    moving["o"] = drain_side("o", moving["o"])
    for b in both:
        d_in = reduce_end(part_b, got_d, b, in_back[b])
        x = tok[b].astype(jnp.float32)
        r_in = rms_scale(x)
        dgt[0:1, :] += jnp.sum(d_in * x * r_in, axis=0, keepdims=True)
        grad_in[b] = dres[b] + norm_backward(d_in, x, r_in, g_attn)
    gains = [send(dgt, dz.at[i], ctx=p) for i, p in enumerate((near, far, other))]
    moving["k"] = drain_side("k", moving["k"])
    out_back[1] = reduce_pass(part_a, got_c, 1, out_back[1])
    moving["v"] = drain_side("v", moving["v"])
    drain_rep("d", moving["d"])
    arrive(gains)
    dsum[...] = dgt[...] + dz[0] + dz[1] + dz[2]
    gains = [send(dsum, dz_s.at[i], shard=p) for i, p in enumerate((sib, opp, dia))]
    moving["q"] = drain_side("q", moving["q"])
    moving["k"] = drain_pair("k", moving["k"])
    moving["v"] = drain_pair("v", moving["v"])
    drain_rep("g", moving["g"])
    arrive(gains)
    dtot[...] = dsum[...] + dz_s[0] + dz_s[1] + dz_s[2]
    gains = [send(dtot, dz_x, rep=1 - r)]
    for b in both:
        total = mixed[b] + reduce_end(part_a, got_c, b, out_back[b])
        block_out[b] = total.astype(jnp.bfloat16)
    for n in "uoqkv":
        drain_rep(n, moving[n])
    arrive(gains)
    gain_out[...] = dtot[...] + dz_x[...]
    for copy in sends:
        if not any(copy is late for late in returned):
            copy.wait_send()


def whole_layer_body(
    tokens,
    positions,
    segments,
    cotangent,
    w_query,
    key_weight,
    value_weight,
    output_weight,
    w_gate,
    w_up,
    w_down,
    norm_gains,
):
    sequences, span, width = tokens.shape
    ctx = lax.axis_size("ctx")
    length = span * ctx
    ff = w_gate.shape[1]
    half = key_weight.shape[1]
    plan, own_total, full_total = row_plan(half, ff)
    heads = 4
    columns = jnp.concatenate([w_query, key_weight, value_weight, w_gate, w_up], axis=1)
    count = norm_gains.shape[0]
    place = lax.axis_index("shard") * ctx + lax.axis_index("ctx")
    all_gains = width * 2 + 2 * HEAD_DIM
    spread_gains = lax.dynamic_update_slice(
        jnp.zeros((all_gains,), jnp.float32), norm_gains.astype(jnp.float32), (place * count,)
    )
    gain_rows = jnp.concatenate(
        [
            spread_gains[:width],
            spread_gains[width + 2 * HEAD_DIM :],
            spread_gains[width : width + 2 * HEAD_DIM],
            jnp.zeros((6 * width - 2 * HEAD_DIM,), jnp.float32),
        ]
    ).reshape(8, width)
    cosine, sine = rope_tables(positions)
    cosine, sine = cosine[:, :, 0], sine[:, :, 0]
    cosine = jnp.concatenate([cosine, cosine], axis=-1)
    sine = jnp.concatenate([-sine, sine], axis=-1)
    bf, f32 = jnp.bfloat16, jnp.float32
    gathered = pltpu.VMEM((sequences, ctx, span, width), bf)
    own_block = pltpu.VMEM((sequences, span, width), bf)
    own_float = pltpu.VMEM((sequences, span, width), f32)
    head_float = pltpu.VMEM((sequences, heads, length, HEAD_DIM), f32)
    head_half = pltpu.VMEM((sequences, heads, length, HEAD_DIM), bf)
    head_lanes = pltpu.VMEM((sequences, length, heads * HEAD_DIM), bf)
    ff_lanes = pltpu.VMEM((sequences, length, heads * ff), bf)
    parts = pltpu.VMEM((ctx, sequences, span, width), bf)
    got = pltpu.VMEM((3, sequences, span, width), bf)
    tile = pltpu.VMEM((8, width), f32)
    tiles_c = pltpu.VMEM((ctx - 1, 8, width), f32)
    tiles_s = pltpu.VMEM((3, 8, width), f32)

    def row_buffer(n):
        return pltpu.VMEM((n, width), bf)

    copies = 128
    vmem = pl.BlockSpec(memory_space=pltpu.VMEM)
    outs = pl.pallas_call(
        functools.partial(layer_kernel, plan),
        out_shape=(
            jax.ShapeDtypeStruct(tokens.shape, bf),
            jax.ShapeDtypeStruct(tokens.shape, f32),
            *(
                jax.ShapeDtypeStruct(weight.shape, f32)
                for weight in (
                    w_query,
                    key_weight,
                    value_weight,
                    output_weight,
                    w_gate,
                    w_up,
                    w_down,
                )
            ),
            jax.ShapeDtypeStruct((8, width), f32),
        ),
        in_specs=[vmem] * 10,
        out_specs=[vmem] * 10,
        scratch_shapes=[
            gathered,
            gathered,
            gathered,
            gathered,
            gathered,
            own_block,
            own_block,
            row_buffer(columns.shape[1]),
            row_buffer(full_total),
            head_float,
            head_float,
            head_half,
            head_half,
            head_half,
            pltpu.VMEM((sequences, heads, length, length), f32),
            head_lanes,
            ff_lanes,
            ff_lanes,
            ff_lanes,
            head_lanes,
            head_lanes,
            head_lanes,
            own_float,
            own_float,
            parts,
            parts,
            got,
            got,
            got,
            got,
            tiles_c,
            tile,
            tiles_s,
            tile,
            tile,
            tiles_c,
            tile,
            tiles_s,
            tile,
            tile,
            row_buffer(full_total),
            row_buffer(full_total // 2),
            row_buffer(full_total // 4),
            row_buffer(full_total // 4),
            pltpu.VMEM((2, HEAD_DIM, width), bf),
            pltpu.VMEM((2, half, width), bf),
            row_buffer(own_total),
            row_buffer(own_total),
            pltpu.SemaphoreType.DMA((copies,)),
            pltpu.SemaphoreType.DMA((copies,)),
        ],
        compiler_params=pltpu.CompilerParams(
            collective_id=0, has_side_effects=True, vmem_limit_bytes=67043328
        ),
    )(
        tokens,
        cotangent,
        columns,
        output_weight,
        w_down,
        gain_rows,
        positions,
        segments,
        cosine,
        sine,
    )
    gains_sum = outs[-1]
    flat = jnp.concatenate([gains_sum[0], gains_sum[2, : 2 * HEAD_DIM], gains_sum[1]])
    return (*outs[:-1], lax.dynamic_slice(flat, (place * count,), (count,)))


def any_body(*arguments):
    tokens, w_query, key_weight, w_gate = (arguments[i] for i in (0, 4, 5, 8))
    ctx, shards = lax.axis_size("ctx"), lax.axis_size("shard")
    fits = w_query.shape[1] == HEAD_DIM and 2 * key_weight.shape[1] == HEAD_DIM
    fits = fits and lax.axis_size("rep") == 2 and shards == 4 and ctx == 4
    fits = fits and w_gate.shape[1] % 64 == 0 and tokens.shape[1] % 16 == 0
    fits = fits and tokens.shape[0] * tokens.shape[1] * ctx <= 512
    if fits:
        return whole_layer_body(*arguments)
    return body(*arguments)


def solution(mesh):
    in_specs = (
        P(("rep", "shard"), "ctx", None),
        P(("rep", "shard"), None),
        P(("rep", "shard"), None),
        P(("rep", "shard"), "ctx", None),
        P(None, ("shard", "ctx")),
        P(None, ("shard", "ctx")),
        P(None, ("shard", "ctx")),
        P(("shard", "ctx"), None),
        P(None, ("shard", "ctx")),
        P(None, ("shard", "ctx")),
        P(("shard", "ctx"), None),
        P(("shard", "ctx")),
    )
    out_specs = (
        P(("rep", "shard"), "ctx", None),
        P(("rep", "shard"), "ctx", None),
        P(None, ("shard", "ctx")),
        P(None, ("shard", "ctx")),
        P(None, ("shard", "ctx")),
        P(("shard", "ctx"), None),
        P(None, ("shard", "ctx")),
        P(None, ("shard", "ctx")),
        P(("shard", "ctx"), None),
        P(("shard", "ctx")),
    )
    return jax.shard_map(any_body, mesh=mesh, in_specs=in_specs, out_specs=out_specs, check_vma=False)
```

```python
import functools
import math

import jax
import jax.numpy as jnp
from jax import lax
from jax.experimental import pallas as pl
from jax.experimental.pallas import tpu as pltpu
from jax.sharding import PartitionSpec as P

QUERY_HEADS = 16
KEY_VALUE_HEADS = 8
HEAD_DIM = 128

MESH = pl.DeviceIdType.MESH

EPSILON = 1e-06
ROPE_BASE = 1000000.0


def rms_scale(values_in):
    return lax.rsqrt(jnp.mean(values_in * values_in, axis=-1, keepdims=True) + EPSILON)


def norm_backward(grad_in, values_in, scale_in, gain_in):
    grad_norm = grad_in * gain_in
    unit = values_in * scale_in
    return scale_in * (grad_norm - unit * jnp.mean(grad_norm * unit, axis=-1, keepdims=True))


def rope_tables(position_ids):
    half_dim = HEAD_DIM // 2
    inverse = 1.0 / ROPE_BASE ** (jnp.arange(half_dim, dtype=jnp.float32) * (2.0 / HEAD_DIM))
    angle = position_ids.astype(jnp.float32)[..., None] * inverse
    return (jnp.cos(angle)[:, :, None, :], jnp.sin(angle)[:, :, None, :])


def rotate(values_in, cosine, sine):
    half_dim = values_in.shape[-1] // 2
    first = values_in[..., :half_dim]
    second = values_in[..., half_dim:]
    return jnp.concatenate(
        [first * cosine - second * sine, second * cosine + first * sine], axis=-1
    )


def rotate_back(grad_in, cosine, sine):
    half_dim = grad_in.shape[-1] // 2
    first = grad_in[..., :half_dim]
    second = grad_in[..., half_dim:]
    return jnp.concatenate(
        [first * cosine + second * sine, second * cosine - first * sine], axis=-1
    )


def float_product(left, right):
    return jnp.dot(left, right, preferred_element_type=jnp.float32)


def against_rows(left, right):
    return lax.dot_general(
        left, right, (((1,), (1,)), ((), ())), preferred_element_type=jnp.float32
    )


def over_tokens(left, right):
    return lax.dot_general(
        left, right, (((0,), (0,)), ((), ())), preferred_element_type=jnp.float32
    )


def body(
    tokens,
    positions,
    segments,
    cotangent,
    w_query,
    key_weight,
    value_weight,
    output_weight,
    w_gate,
    w_up,
    w_down,
    norm_gains,
):
    sequence_count, local_length, model_width = tokens.shape
    total_rows = sequence_count * local_length
    group_width = QUERY_HEADS // KEY_VALUE_HEADS
    score_scale = 1.0 / math.sqrt(HEAD_DIM)
    local_start = lax.axis_index("ctx") * local_length
    local_pos = lax.dynamic_slice_in_dim(positions, local_start, local_length, 1)
    local_seg = lax.dynamic_slice_in_dim(segments, local_start, local_length, 1)
    wq_full, full_key_weight, full_value_weight, wo_full, gains_full = (
        lax.all_gather(w_query, ("shard", "ctx"), axis=1, tiled=True),
        lax.all_gather(key_weight, ("shard", "ctx"), axis=1, tiled=True),
        lax.all_gather(value_weight, ("shard", "ctx"), axis=1, tiled=True),
        lax.all_gather(output_weight, ("shard", "ctx"), axis=0, tiled=True),
        lax.all_gather(norm_gains, ("shard", "ctx"), axis=0, tiled=True),
    )
    gain_all = gains_full.astype(jnp.float32)
    g_attn = gain_all[:model_width]
    g_query = gain_all[model_width : model_width + HEAD_DIM]
    key_gain = gain_all[model_width + HEAD_DIM : model_width + 2 * HEAD_DIM]
    g_mlp = gain_all[model_width + 2 * HEAD_DIM :]
    x_rows = tokens.reshape(total_rows, model_width).astype(jnp.float32)
    scale_in = rms_scale(x_rows)
    normed_input = (x_rows * scale_in * g_attn).astype(jnp.bfloat16)
    query = float_product(normed_input, wq_full).reshape(
        sequence_count, local_length, QUERY_HEADS, HEAD_DIM
    )
    key_rows = float_product(normed_input, full_key_weight).reshape(
        sequence_count, local_length, KEY_VALUE_HEADS, HEAD_DIM
    )
    value_rows = (
        float_product(normed_input, full_value_weight)
        .astype(jnp.bfloat16)
        .reshape(sequence_count, local_length, KEY_VALUE_HEADS, HEAD_DIM)
    )
    q_scale = rms_scale(query)
    key_scale = rms_scale(key_rows)
    cosine, sine = rope_tables(local_pos)
    query_rotated = rotate(query * q_scale * g_query, cosine, sine).astype(jnp.bfloat16)
    k_rot = rotate(key_rows * key_scale * key_gain, cosine, sine).astype(jnp.bfloat16)
    keys_all, values_all = (
        lax.all_gather(k_rot, "ctx", axis=1, tiled=True),
        lax.all_gather(value_rows, "ctx", axis=1, tiled=True),
    )
    allowed = (
        (local_seg[:, :, None] == segments[:, None, :])
        & (positions[:, None, :] <= local_pos[:, :, None])
    )[:, None, None]
    query_group = query_rotated.reshape(
        sequence_count, local_length, KEY_VALUE_HEADS, group_width, HEAD_DIM
    )
    scores = (
        jnp.einsum("bqkgd,bskd->bkgqs", query_group, keys_all, preferred_element_type=jnp.float32)
        * score_scale
    )
    exponent = jnp.where(allowed, jnp.exp(scores), 0.0)
    denominator = jnp.sum(exponent, axis=-1)
    log_total = jnp.log(denominator)
    probs = (exponent / denominator[..., None]).astype(jnp.bfloat16)
    attention_output = jnp.einsum(
        "bkgqs,bskd->bqkgd", probs, values_all, preferred_element_type=jnp.float32
    )
    attention_output = attention_output.astype(jnp.bfloat16).reshape(
        total_rows, QUERY_HEADS * HEAD_DIM
    )
    mixed_in = x_rows + float_product(attention_output, wo_full)
    scale_mid = rms_scale(mixed_in)
    normed_mid = (mixed_in * scale_mid * g_mlp).astype(jnp.bfloat16)
    wg_full, wu_full, wd_full = (
        lax.all_gather(w_gate, ("shard", "ctx"), axis=1, tiled=True),
        lax.all_gather(w_up, ("shard", "ctx"), axis=1, tiled=True),
        lax.all_gather(w_down, ("shard", "ctx"), axis=0, tiled=True),
    )
    gate_pre = float_product(normed_mid, wg_full)
    up_pre = float_product(normed_mid, wu_full)
    sigmoid_gate = jax.nn.sigmoid(gate_pre)
    hidden = (gate_pre * sigmoid_gate * up_pre).astype(jnp.bfloat16)
    block_sum = mixed_in + float_product(hidden, wd_full)
    block_out = block_sum.astype(jnp.bfloat16).reshape(sequence_count, local_length, model_width)
    grad_rows = cotangent.reshape(total_rows, model_width)
    d_hidden = against_rows(grad_rows, wd_full)
    grad_down = over_tokens(hidden, grad_rows)
    d_gate = (d_hidden * up_pre * sigmoid_gate * (1.0 + gate_pre * (1.0 - sigmoid_gate))).astype(
        jnp.bfloat16
    )
    d_up = (d_hidden * gate_pre * sigmoid_gate).astype(jnp.bfloat16)
    grad_gate = over_tokens(normed_mid, d_gate)
    grad_up = over_tokens(normed_mid, d_up)
    owned_gate, owned_up, owned_down = (
        lax.psum_scatter(grad_gate, ("shard", "ctx"), scatter_dimension=1, tiled=True),
        lax.psum_scatter(grad_up, ("shard", "ctx"), scatter_dimension=1, tiled=True),
        lax.psum_scatter(grad_down, ("shard", "ctx"), scatter_dimension=0, tiled=True),
    )
    total_gate, total_up, total_down = (
        lax.psum(owned_gate.astype(jnp.bfloat16), "rep").astype(jnp.float32),
        lax.psum(owned_up.astype(jnp.bfloat16), "rep").astype(jnp.float32),
        lax.psum(owned_down.astype(jnp.bfloat16), "rep").astype(jnp.float32),
    )
    d_mid = against_rows(d_gate, wg_full) + against_rows(d_up, wu_full)
    dg_mlp = jnp.sum(d_mid * mixed_in * scale_mid, axis=0)
    d_resid = grad_rows.astype(jnp.float32) + norm_backward(d_mid, mixed_in, scale_mid, g_mlp)
    residual_gradient_bfloat = d_resid.astype(jnp.bfloat16)
    grad_output = over_tokens(attention_output, residual_gradient_bfloat)
    attention_gradient = (
        against_rows(residual_gradient_bfloat, wo_full)
        .astype(jnp.bfloat16)
        .reshape(sequence_count, local_length, KEY_VALUE_HEADS, group_width, HEAD_DIM)
    )
    attention_heads = attention_output.reshape(
        sequence_count, local_length, KEY_VALUE_HEADS, group_width, HEAD_DIM
    )
    row_delta = jnp.sum(
        attention_gradient.astype(jnp.float32) * attention_heads.astype(jnp.float32), axis=-1
    )
    row_delta = jnp.transpose(row_delta, (0, 2, 3, 1))
    scores_again = (
        jnp.einsum("bqkgd,bskd->bkgqs", query_group, keys_all, preferred_element_type=jnp.float32)
        * score_scale
    )
    probs_back = jnp.where(allowed, jnp.exp(scores_again - log_total[..., None]), 0.0)
    probs_round = probs_back.astype(jnp.bfloat16)
    values_gradient = jnp.einsum(
        "bkgqs,bqkgd->bskd", probs_round, attention_gradient, preferred_element_type=jnp.float32
    )
    d_probs = jnp.einsum(
        "bqkgd,bskd->bkgqs", attention_gradient, values_all, preferred_element_type=jnp.float32
    )
    d_scores = (probs_back * (d_probs - row_delta[..., None])).astype(jnp.bfloat16)
    d_qrot = (
        jnp.einsum("bkgqs,bskd->bqkgd", d_scores, keys_all, preferred_element_type=jnp.float32)
        * score_scale
    )
    d_krot = (
        jnp.einsum("bkgqs,bqkgd->bskd", d_scores, query_group, preferred_element_type=jnp.float32)
        * score_scale
    )
    d_keys, value_rows_gradient = (
        lax.psum_scatter(
            d_krot.astype(jnp.bfloat16), "ctx", scatter_dimension=1, tiled=True
        ).astype(jnp.float32),
        lax.psum_scatter(
            values_gradient.astype(jnp.bfloat16), "ctx", scatter_dimension=1, tiled=True
        ).astype(jnp.float32),
    )
    d_qn = rotate_back(
        d_qrot.reshape(sequence_count, local_length, QUERY_HEADS, HEAD_DIM), cosine, sine
    )
    normed_key_gradient = rotate_back(d_keys, cosine, sine)
    dg_query = jnp.sum(d_qn * query * q_scale, axis=(0, 1, 2))
    dg_key = jnp.sum(normed_key_gradient * key_rows * key_scale, axis=(0, 1, 2))
    d_query = (
        norm_backward(d_qn, query, q_scale, g_query)
        .astype(jnp.bfloat16)
        .reshape(total_rows, QUERY_HEADS * HEAD_DIM)
    )
    key_gradient = (
        norm_backward(normed_key_gradient, key_rows, key_scale, key_gain)
        .astype(jnp.bfloat16)
        .reshape(total_rows, KEY_VALUE_HEADS * HEAD_DIM)
    )
    value_gradient = value_rows_gradient.astype(jnp.bfloat16).reshape(
        total_rows, KEY_VALUE_HEADS * HEAD_DIM
    )
    grad_query = over_tokens(normed_input, d_query)
    grad_key = over_tokens(normed_input, key_gradient)
    grad_value = over_tokens(normed_input, value_gradient)
    d_in = (
        against_rows(d_query, wq_full)
        + against_rows(key_gradient, full_key_weight)
        + against_rows(value_gradient, full_value_weight)
    )
    dg_attn = jnp.sum(d_in * x_rows * scale_in, axis=0)
    grad_input = (d_resid + norm_backward(d_in, x_rows, scale_in, g_attn)).reshape(
        sequence_count, local_length, model_width
    )
    grad_gains = jnp.concatenate([dg_attn, dg_query, dg_key, dg_mlp])
    owned_query, owned_key, owned_value, owned_output, owned_gains = (
        lax.psum_scatter(grad_query, ("shard", "ctx"), scatter_dimension=1, tiled=True),
        lax.psum_scatter(grad_key, ("shard", "ctx"), scatter_dimension=1, tiled=True),
        lax.psum_scatter(grad_value, ("shard", "ctx"), scatter_dimension=1, tiled=True),
        lax.psum_scatter(grad_output, ("shard", "ctx"), scatter_dimension=0, tiled=True),
        lax.psum_scatter(grad_gains, ("shard", "ctx"), scatter_dimension=0, tiled=True),
    )
    total_query, total_key, total_value, total_output, total_gains = (
        lax.psum(owned_query.astype(jnp.bfloat16), "rep").astype(jnp.float32),
        lax.psum(owned_key.astype(jnp.bfloat16), "rep").astype(jnp.float32),
        lax.psum(owned_value.astype(jnp.bfloat16), "rep").astype(jnp.float32),
        lax.psum(owned_output.astype(jnp.bfloat16), "rep").astype(jnp.float32),
        lax.psum(owned_gains.astype(jnp.bfloat16), "rep").astype(jnp.float32),
    )
    return (
        block_out,
        grad_input,
        total_query,
        total_key,
        total_value,
        total_output,
        total_gate,
        total_up,
        total_down,
        total_gains,
    )


def row_plan(head_half, ff):
    sizes = (
        ("q", HEAD_DIM, HEAD_DIM),
        ("k", head_half, HEAD_DIM),
        ("v", head_half, HEAD_DIM),
        ("o", HEAD_DIM, HEAD_DIM),
        ("g", ff, ff),
        ("u", ff, ff),
        ("d", ff, ff),
    )
    plan, own, full = {}, 0, 0
    for name, own_rows, block_rows in sizes:
        plan[name] = (own, own_rows, full, block_rows)
        own, full = own + own_rows, full + 4 * block_rows
    return plan, own, full


def plain(left, right):
    return lax.dot_general(left, right, (((1,), (0,)), ((), ())), preferred_element_type=jnp.float32)


def swap_halves(values_in):
    return pltpu.roll(values_in, values_in.shape[-1] // 2, 1)


def rows(start, size, step):
    return pl.ds(pl.multiple_of(start, step), size)


def hand_over(*refs):
    count = len(refs) // 2
    for src, dst in zip(refs[:count], refs[count:]):
        dst[...] = src[...]


def layer_kernel(
    plan,
    tok,
    cot,
    w_q,
    k_rows,
    v_rows,
    out_rows,
    gate_rows,
    up_rows,
    down_rows,
    gain_in,
    pos,
    seg,
    cosine,
    sine,
    block_out,
    grad_in,
    grad_q,
    grad_k,
    grad_v,
    grad_o,
    grad_g,
    grad_u,
    grad_d,
    gain_out,
    x_all,
    c_all,
    nx,
    nm,
    res,
    own_mid,
    own_res,
    wb,
    qf,
    kf,
    qr,
    kr,
    vb,
    prob,
    att,
    hid,
    dga,
    dup,
    dqb,
    dkb,
    dvb,
    mixed,
    dres,
    part_a,
    part_b,
    got_a,
    got_b,
    got_c,
    got_d,
    gz,
    gsum,
    gz_s,
    gfull,
    dgt,
    dz,
    dsum,
    dz_s,
    dtot,
    dz_x,
    gb,
    rk,
    hs,
    ry,
    kvh,
    kvr,
    xo,
    rx,
    send_sem,
    recv_sem,
):
    sequences, span, width = tok.shape
    ctx = lax.axis_size("ctx")
    length = span * ctx
    heads = 4
    scale = 1.0 / math.sqrt(HEAD_DIM)
    r, s, c = lax.axis_index("rep"), lax.axis_index("shard"), lax.axis_index("ctx")
    core, side = s % 2, s // 2
    sib, opp = s + 1 - 2 * core, (s + 2) % 4
    dia = (sib + 2) % 4
    mine, theirs = core * 2 + side, core * 2 + 1 - side
    half = c % 2
    near = c + 1 - 2 * half
    far = (c + 2) % 4
    other = (near + 2) % 4
    both = range(sequences)
    sends, lent, returned = [], [], []

    def send(src, dst, **where):
        at = len(sends)
        copy = pltpu.make_async_remote_copy(
            src_ref=src,
            dst_ref=dst,
            send_sem=send_sem.at[at],
            recv_sem=recv_sem.at[at],
            device_id=where,
            device_id_type=MESH,
        )
        copy.start()
        sends.append(copy)
        return copy

    def arrive(copies):
        for copy in copies:
            copy.wait_recv()

    def reclaim(copies):
        for copy in copies:
            copy.wait_send()
            returned.append(copy)

    def gather_start(src, dst, b):
        dst[b, c] = src[b]
        across = send(src.at[b], dst.at[b, c], ctx=far)
        beside = send(src.at[b], dst.at[b, c], ctx=near)
        return beside, across

    def gather_pass(dst, b, pair):
        arrive([pair[1]])
        return pair[0], send(dst.at[b, far], dst.at[b, far], ctx=near)

    def reduce_start(src, got, b):
        first = send(src.at[other, b], got.at[0, b], ctx=near)
        second = send(src.at[near, b], got.at[1, b], ctx=near)
        lent.extend((first, second))
        return first, second

    def reduce_pass(src, got, b, pair):
        arrive([pair[0]])
        total = src[far, b].astype(jnp.float32) + got[0, b].astype(jnp.float32)
        src[far, b] = total.astype(jnp.bfloat16)
        third = send(src.at[far, b], got.at[2, b], ctx=far)
        lent.append(third)
        return pair[1], third

    def reduce_end(src, got, b, pair):
        arrive(pair)
        total = src[c, b].astype(jnp.float32) + got[1, b].astype(jnp.float32)
        return total + got[2, b].astype(jnp.float32)

    def block(name, at):
        _, _, off, size = plan[name]
        return rows(off + at * size, size, 64)

    def spread_rows(own):
        there = send(wb.at[own], wb.at[own], shard=opp)
        return [there], [send(wb.at[own], wb.at[own], shard=sib)]

    def spread(name):
        return spread_rows(block(name, mine))

    def pass_on(name):
        got = block(name, theirs)
        return send(wb.at[got], wb.at[got], shard=sib)

    def own_rows(name):
        off, size = plan[name][:2]
        return pl.ds(off, size)

    def matrix(name):
        _, _, off, size = plan[name]
        return wb[pl.ds(off, 4 * size), :]

    def whole(ref, b):
        return ref[b].reshape(length, width)

    def split(values_in, dst, b):
        for j in range(ctx):
            dst[j, b] = values_in[j * span : (j + 1) * span].astype(jnp.bfloat16)

    barrier = pltpu.get_barrier_semaphore()
    peers = [{"ctx": near}, {"ctx": far}, {"ctx": other}]
    peers += [{"shard": sib}, {"shard": opp}, {"shard": dia}, {"rep": 1 - r}]
    for peer in peers:
        pl.semaphore_signal(barrier, inc=1, device_id=peer, device_id_type=MESH)
    pl.semaphore_wait(barrier, len(peers))

    head_half = plan["k"][1]
    gains = [send(gain_in, gz.at[i], ctx=p) for i, p in enumerate((near, far, other))]
    kv_in, spreads = [], {}
    for n, src in zip("kv", (k_rows, v_rows)):
        first = plan[n][2] + mine * HEAD_DIM
        at = rows(first + half * head_half, head_half, 64)
        wb[at, :] = src[...]
        kv_in.append(send(wb.at[at], wb.at[at], ctx=near))
        spreads[n] = spread_rows(at)
    tok_in = [gather_start(tok, x_all, b) for b in both]
    wb[block("q", mine), :] = w_q[...].astype(jnp.float32).T.astype(jnp.bfloat16)
    for n, src in zip("ogud", (out_rows, gate_rows, up_rows, down_rows)):
        wb[block(n, mine), :] = src[...]
    arrive(gains)
    gsum[...] = gain_in[...] + gz[0] + gz[1] + gz[2]
    gains = [send(gsum, gz_s.at[i], shard=p) for i, p in enumerate((sib, opp, dia))]
    spreads["q"] = spread("q")
    arrive(kv_in)
    for n in "kv":
        first = plan[n][2] + mine * HEAD_DIM
        late = spread_rows(rows(first + (1 - half) * head_half, head_half, 64))
        for early, more in zip(spreads[n], late):
            early.extend(more)
    spreads["o"] = spread("o")
    arrive(gains)
    gfull[...] = gsum[...] + gz_s[0] + gz_s[1] + gz_s[2]
    g_attn = gfull[0:1, :]
    g_mlp = gfull[1:2, :]
    g_query = gfull[2:3, :HEAD_DIM]
    g_key = gfull[2:3, HEAD_DIM : 2 * HEAD_DIM]
    passed = {}

    def pass_weights(names):
        for n in names:
            arrive(spreads[n][0])
            passed[n] = pass_on(n)

    def have_weights(names):
        for n in names:
            arrive(spreads[n][1] + [passed[n]])

    tok_in[0] = gather_pass(x_all, 0, tok_in[0])
    pass_weights("qkv")
    tok_in[1] = gather_pass(x_all, 1, tok_in[1])
    cot_in = [gather_start(cot, c_all, 0)]

    def norm_rows(b):
        def one(j, carry):
            x = x_all[b, j].astype(jnp.float32)
            nx[b, j] = (x * rms_scale(x) * g_attn).astype(jnp.bfloat16)
            return carry

        lax.fori_loop(0, ctx, one, 0)

    def attend(b):
        x = whole(nx, b)
        query = against_rows(x, matrix("q"))
        key = against_rows(x, matrix("k"))
        value = against_rows(x, matrix("v")).astype(jnp.bfloat16)
        cos_b, sin_b = cosine[b], sine[b]
        key_at = jnp.broadcast_to(pos[b : b + 1, :].astype(jnp.float32), (length, length))
        key_doc = jnp.broadcast_to(seg[b : b + 1, :].astype(jnp.float32), (length, length))
        allowed = (key_doc.T == key_doc) & (key_at <= key_at.T)
        for h in range(heads):
            at = slice(h * HEAD_DIM, (h + 1) * HEAD_DIM)
            q, k, v = query[:, at], key[:, at], value[:, at]
            qn = q * rms_scale(q) * g_query
            kn = k * rms_scale(k) * g_key
            q_rot = (qn * cos_b + swap_halves(qn) * sin_b).astype(jnp.bfloat16)
            k_rot = (kn * cos_b + swap_halves(kn) * sin_b).astype(jnp.bfloat16)
            qf[b, h], kf[b, h] = q, k
            qr[b, h], kr[b, h], vb[b, h] = q_rot, k_rot, v
            scores = against_rows(q_rot, k_rot) * scale
            exponent = jnp.where(allowed, jnp.exp(scores), 0.0)
            p = exponent / jnp.sum(exponent, axis=-1, keepdims=True)
            prob[b, h] = p
            att[b, :, at] = plain(p.astype(jnp.bfloat16), v).astype(jnp.bfloat16)

    out_part = []
    for b in both:
        arrive(tok_in[b])
        norm_rows(b)
        if b == 0:
            have_weights("qkv")
        else:
            for n in "gud":
                spreads[n] = spread(n)
        attend(b)
        if b == 0:
            pass_weights("o")
            have_weights("o")
        else:
            out_part[0] = reduce_pass(part_a, got_a, 0, out_part[0])
        split(plain(att[b], matrix("o")), part_a, b)
        out_part.append(reduce_start(part_a, got_a, b))
        if b == 0:
            cot_in.append(gather_start(cot, c_all, 1))
    out_part[1] = reduce_pass(part_a, got_a, 1, out_part[1])
    first_parts = list(lent)
    mid_in = []
    for b in both:
        m = tok[b].astype(jnp.float32) + reduce_end(part_a, got_a, b, out_part[b])
        mixed[b] = m
        own_mid[b] = (m * rms_scale(m) * g_mlp).astype(jnp.bfloat16)
        mid_in.append(gather_start(own_mid, nm, b))
        cot_in[b] = gather_pass(c_all, b, cot_in[b])
    pass_weights("gud")
    mid_in = [gather_pass(nm, b, mid_in[b]) for b in both]
    have_weights("gud")

    def feed(b):
        n, ct = whole(nm, b), whole(c_all, b)
        gate = against_rows(n, matrix("g"))
        up = against_rows(n, matrix("u"))
        d_hidden = against_rows(ct, matrix("d"))
        sig = jax.nn.sigmoid(gate)
        hid[b] = (gate * sig * up).astype(jnp.bfloat16)
        d_gate = (d_hidden * up * sig * (1.0 + gate * (1.0 - sig))).astype(jnp.bfloat16)
        d_up = (d_hidden * gate * sig).astype(jnp.bfloat16)
        dga[b], dup[b] = d_gate, d_up
        split(plain(d_gate, matrix("g")) + plain(d_up, matrix("u")), part_b, b)

    mid_back = []
    for b in both:
        arrive(cot_in[b])
        arrive(mid_in[b])
        feed(b)
        mid_back.append(reduce_start(part_b, got_b, b))

    def weigh(name, left, right):
        _, _, off, size = plan[name]
        right = right[...].reshape(sequences * length, width)
        chunk = 256

        def some(i, carry):
            at = pl.multiple_of(i * chunk, chunk)
            lhs = left[:, :, pl.ds(at, chunk)].reshape(sequences * length, chunk)
            gb[rows(off + at, chunk, 64), :] = over_tokens(lhs, right).astype(jnp.bfloat16)
            return carry

        lax.fori_loop(0, 4 * size // chunk, some, 0)
        return send(
            gb.at[rows(off + (1 - core) * 2 * size, 2 * size, 64)],
            rk.at[pl.ds(off // 2, 2 * size)],
            shard=sib,
        )

    def core_sum(name, at):
        _, _, off, size = plan[name]
        here = gb[rows(off + (core * 2 + at) * size, size, 64), :]
        there = rk[rows(off // 2 + at * size, size, 64), :]
        return here.astype(jnp.float32) + there.astype(jnp.float32)

    def drain_core(name, copy):
        _, _, off, size = plan[name]
        arrive([copy])
        at = pl.ds(off // 4, size)
        hs[at, :] = core_sum(name, 1 - side).astype(jnp.bfloat16)
        return send(hs.at[at], ry.at[at], shard=opp)

    def drain_side(name, copy):
        own, own_size, off, size = plan[name]
        arrive([copy])
        total = core_sum(name, side) + ry[pl.ds(off // 4, size), :].astype(jnp.float32)
        total = total.astype(jnp.bfloat16)
        at = pl.ds(own, own_size)
        if own_size == size:
            xo[at, :] = total
            return send(xo.at[at], rx.at[at], rep=1 - r)
        i = "kv".index(name)
        kvh[i] = total
        return send(kvh.at[i, rows((1 - half) * own_size, own_size, 64)], kvr.at[i], ctx=near)

    def drain_pair(name, copy):
        own, own_size, _, _ = plan[name]
        arrive([copy])
        i = "kv".index(name)
        total = kvh[i, rows(half * own_size, own_size, 64), :].astype(jnp.float32)
        at = pl.ds(own, own_size)
        xo[at, :] = (total + kvr[i].astype(jnp.float32)).astype(jnp.bfloat16)
        return send(xo.at[at], rx.at[at], rep=1 - r)

    results = dict(zip("qkvogud", (grad_q, grad_k, grad_v, grad_o, grad_g, grad_u, grad_d)))

    def drain_rep(name, copy):
        at = own_rows(name)
        arrive([copy])
        total = xo[at, :].astype(jnp.float32) + rx[at, :].astype(jnp.float32)
        out = results[name]
        out[...] = total.T if name == "q" else total

    dgt[...] = jnp.zeros_like(dgt)
    res_in = []

    def enter(b):
        d_mid = reduce_end(part_b, got_b, b, mid_back[b])
        m = mixed[b]
        r_mid = rms_scale(m)
        dgt[1:2, :] += jnp.sum(d_mid * m * r_mid, axis=0, keepdims=True)
        d_resid = cot[b].astype(jnp.float32) + norm_backward(d_mid, m, r_mid, g_mlp)
        dres[b] = d_resid
        own_res[b] = d_resid.astype(jnp.bfloat16)
        res_in.append(gather_start(own_res, res, b))

    reclaim(first_parts)
    moving = {}
    moving["d"] = weigh("d", hid, c_all)
    moving["g"] = weigh("g", dga, nm)
    moving["d"] = drain_core("d", moving["d"])
    mid_back[0] = reduce_pass(part_b, got_b, 0, mid_back[0])
    moving["u"] = weigh("u", dup, nm)
    moving["g"] = drain_core("g", moving["g"])
    mid_back[1] = reduce_pass(part_b, got_b, 1, mid_back[1])
    second_parts = lent[len(first_parts) :]
    enter(0)
    moving["u"] = drain_core("u", moving["u"])
    enter(1)
    moving["d"] = drain_side("d", moving["d"])
    for b in both:
        split(plain(hid[b], matrix("d")), part_a, b)
    res_in = [gather_pass(res, b, res_in[b]) for b in both]
    out_back = [reduce_start(part_a, got_c, b) for b in both]
    reclaim(second_parts)

    def attend_back(b):
        d_att = against_rows(whole(res, b), matrix("o")).astype(jnp.bfloat16)
        cos_b, sin_b = cosine[b], sine[b]

        def through(d_rot, u, gain):
            d_n = d_rot * cos_b - swap_halves(d_rot) * sin_b
            u_scale = rms_scale(u)
            gain_row = jnp.sum(d_n * u * u_scale, axis=0, keepdims=True)
            return norm_backward(d_n, u, u_scale, gain).astype(jnp.bfloat16), gain_row

        for h in range(heads):
            at = slice(h * HEAD_DIM, (h + 1) * HEAD_DIM)
            da, p = d_att[:, at], prob[b, h]
            delta = jnp.sum(
                da.astype(jnp.float32) * att[b, :, at].astype(jnp.float32), axis=-1, keepdims=True
            )
            dvb[b, :, at] = over_tokens(p.astype(jnp.bfloat16), da).astype(jnp.bfloat16)
            d_p = against_rows(da, vb[b, h])
            d_s = (p * (d_p - delta)).astype(jnp.bfloat16)
            d_q, row_q = through(plain(d_s, kr[b, h]) * scale, qf[b, h], g_query)
            d_k, row_k = through(over_tokens(d_s, qr[b, h]) * scale, kf[b, h], g_key)
            dqb[b, :, at] = d_q
            dkb[b, :, at] = d_k
            dgt[2:3, :HEAD_DIM] += row_q
            dgt[2:3, HEAD_DIM : 2 * HEAD_DIM] += row_k
        d_in = plain(dqb[b], matrix("q")) + plain(dkb[b], matrix("k")) + plain(dvb[b], matrix("v"))
        split(d_in, part_b, b)

    arrive(res_in[0])
    moving["g"] = drain_side("g", moving["g"])
    attend_back(0)
    in_back = [reduce_start(part_b, got_d, 0)]
    out_back[0] = reduce_pass(part_a, got_c, 0, out_back[0])
    arrive(res_in[1])
    moving["o"] = weigh("o", att, res)
    moving["u"] = drain_side("u", moving["u"])
    moving["o"] = drain_core("o", moving["o"])
    attend_back(1)
    in_back.append(reduce_start(part_b, got_d, 1))
    out_back[1] = reduce_pass(part_a, got_c, 1, out_back[1])
    moving["k"] = weigh("k", dkb, nx)
    moving["v"] = weigh("v", dvb, nx)
    moving["k"] = drain_core("k", moving["k"])
    in_back[0] = reduce_pass(part_b, got_d, 0, in_back[0])
    moving["q"] = weigh("q", dqb, nx)
    moving["v"] = drain_core("v", moving["v"])
    moving["o"] = drain_side("o", moving["o"])
    moving["q"] = drain_core("q", moving["q"])
    in_back[1] = reduce_pass(part_b, got_d, 1, in_back[1])
    moving["k"] = drain_side("k", moving["k"])
    for b in both:
        d_in = reduce_end(part_b, got_d, b, in_back[b])
        x = tok[b].astype(jnp.float32)
        r_in = rms_scale(x)
        dgt[0:1, :] += jnp.sum(d_in * x * r_in, axis=0, keepdims=True)
        grad_in[b] = dres[b] + norm_backward(d_in, x, r_in, g_attn)
    gains = [send(dgt, dz.at[i], ctx=p) for i, p in enumerate((near, far, other))]
    moving["v"] = drain_side("v", moving["v"])
    moving["k"] = drain_pair("k", moving["k"])
    arrive(gains)
    dsum[...] = dgt[...] + dz[0] + dz[1] + dz[2]
    gains = [send(dsum, dz_s.at[i], shard=p) for i, p in enumerate((sib, opp, dia))]
    moving["q"] = drain_side("q", moving["q"])
    moving["v"] = drain_pair("v", moving["v"])
    drain_rep("d", moving["d"])
    drain_rep("g", moving["g"])
    arrive(gains)
    dtot[...] = dsum[...] + dz_s[0] + dz_s[1] + dz_s[2]
    gains = [send(dtot, dz_x, rep=1 - r)]
    for b in both:
        total = mixed[b] + reduce_end(part_a, got_c, b, out_back[b])
        block_out[b] = total.astype(jnp.bfloat16)
    for n in "uokqv":
        drain_rep(n, moving[n])
    arrive(gains)
    gain_out[...] = dtot[...] + dz_x[...]
    for copy in sends:
        if not any(copy is late for late in returned):
            copy.wait_send()


def whole_layer_body(
    tokens,
    positions,
    segments,
    cotangent,
    w_query,
    key_weight,
    value_weight,
    output_weight,
    w_gate,
    w_up,
    w_down,
    norm_gains,
):
    sequences, span, width = tokens.shape
    ctx = lax.axis_size("ctx")
    length = span * ctx
    ff = w_gate.shape[1]
    half = key_weight.shape[1]
    plan, own_total, full_total = row_plan(half, ff)
    heads = 4
    k_rows, v_rows, g_rows, u_rows = key_weight.T, value_weight.T, w_gate.T, w_up.T
    count = norm_gains.shape[0]
    place = lax.axis_index("shard") * ctx + lax.axis_index("ctx")
    all_gains = width * 2 + 2 * HEAD_DIM
    spread_gains = lax.dynamic_update_slice(
        jnp.zeros((all_gains,), jnp.float32), norm_gains.astype(jnp.float32), (place * count,)
    )
    gain_rows = jnp.concatenate(
        [
            spread_gains[:width],
            spread_gains[width + 2 * HEAD_DIM :],
            spread_gains[width : width + 2 * HEAD_DIM],
            jnp.zeros((6 * width - 2 * HEAD_DIM,), jnp.float32),
        ]
    ).reshape(8, width)
    cosine, sine = rope_tables(positions)
    cosine, sine = cosine[:, :, 0], sine[:, :, 0]
    cosine = jnp.concatenate([cosine, cosine], axis=-1)
    sine = jnp.concatenate([-sine, sine], axis=-1)
    bf, f32 = jnp.bfloat16, jnp.float32
    gathered = pltpu.VMEM((sequences, ctx, span, width), bf)
    own_block = pltpu.VMEM((sequences, span, width), bf)
    own_float = pltpu.VMEM((sequences, span, width), f32)
    head_float = pltpu.VMEM((sequences, heads, length, HEAD_DIM), f32)
    head_half = pltpu.VMEM((sequences, heads, length, HEAD_DIM), bf)
    head_lanes = pltpu.VMEM((sequences, length, heads * HEAD_DIM), bf)
    ff_lanes = pltpu.VMEM((sequences, length, heads * ff), bf)
    parts = pltpu.VMEM((ctx, sequences, span, width), bf)
    got = pltpu.VMEM((3, sequences, span, width), bf)
    tile = pltpu.VMEM((8, width), f32)
    tiles_c = pltpu.VMEM((ctx - 1, 8, width), f32)
    tiles_s = pltpu.VMEM((3, 8, width), f32)

    def row_buffer(n):
        return pltpu.VMEM((n, width), bf)

    copies = 128
    vmem = pl.BlockSpec(memory_space=pltpu.VMEM)
    outs = pl.pallas_call(
        functools.partial(layer_kernel, plan),
        out_shape=(
            jax.ShapeDtypeStruct(tokens.shape, bf),
            jax.ShapeDtypeStruct(tokens.shape, f32),
            *(
                jax.ShapeDtypeStruct(weight.shape, f32)
                for weight in (
                    w_query,
                    k_rows,
                    v_rows,
                    output_weight,
                    g_rows,
                    u_rows,
                    w_down,
                )
            ),
            jax.ShapeDtypeStruct((8, width), f32),
        ),
        in_specs=[vmem] * 14,
        out_specs=[vmem] * 10,
        scratch_shapes=[
            gathered,
            gathered,
            gathered,
            gathered,
            gathered,
            own_block,
            own_block,
            row_buffer(full_total),
            head_float,
            head_float,
            head_half,
            head_half,
            head_half,
            pltpu.VMEM((sequences, heads, length, length), f32),
            head_lanes,
            ff_lanes,
            ff_lanes,
            ff_lanes,
            head_lanes,
            head_lanes,
            head_lanes,
            own_float,
            own_float,
            parts,
            parts,
            got,
            got,
            got,
            got,
            tiles_c,
            tile,
            tiles_s,
            tile,
            tile,
            tiles_c,
            tile,
            tiles_s,
            tile,
            tile,
            row_buffer(full_total),
            row_buffer(full_total // 2),
            row_buffer(full_total // 4),
            row_buffer(full_total // 4),
            pltpu.VMEM((2, HEAD_DIM, width), bf),
            pltpu.VMEM((2, half, width), bf),
            row_buffer(own_total),
            row_buffer(own_total),
            pltpu.SemaphoreType.DMA((copies,)),
            pltpu.SemaphoreType.DMA((copies,)),
        ],
        compiler_params=pltpu.CompilerParams(
            collective_id=0, has_side_effects=True, vmem_limit_bytes=67043328
        ),
    )(
        tokens,
        cotangent,
        w_query,
        k_rows,
        v_rows,
        output_weight,
        g_rows,
        u_rows,
        w_down,
        gain_rows,
        positions,
        segments,
        cosine,
        sine,
    )
    outs = pl.pallas_call(
        hand_over,
        out_shape=[jax.ShapeDtypeStruct(out.shape, out.dtype) for out in outs],
        in_specs=[vmem] * len(outs),
        out_specs=[vmem] * len(outs),
    )(*outs)
    block_out, grad_input, d_q, d_k, d_v, d_o, d_g, d_u, d_d, gains_sum = outs
    flat = jnp.concatenate([gains_sum[0], gains_sum[2, : 2 * HEAD_DIM], gains_sum[1]])
    own_gains = lax.dynamic_slice(flat, (place * count,), (count,))
    return (block_out, grad_input, d_q, d_k.T, d_v.T, d_o, d_g.T, d_u.T, d_d, own_gains)


def any_body(*arguments):
    tokens, w_query, key_weight, w_gate = (arguments[i] for i in (0, 4, 5, 8))
    ctx, shards = lax.axis_size("ctx"), lax.axis_size("shard")
    fits = w_query.shape[1] == HEAD_DIM and 2 * key_weight.shape[1] == HEAD_DIM
    fits = fits and lax.axis_size("rep") == 2 and shards == 4 and ctx == 4
    fits = fits and w_gate.shape[1] % 64 == 0 and tokens.shape[1] % 16 == 0
    fits = fits and tokens.shape[0] * tokens.shape[1] * ctx <= 512
    if fits:
        return whole_layer_body(*arguments)
    return body(*arguments)


def solution(mesh):
    in_specs = (
        P(("rep", "shard"), "ctx", None),
        P(("rep", "shard"), None),
        P(("rep", "shard"), None),
        P(("rep", "shard"), "ctx", None),
        P(None, ("shard", "ctx")),
        P(None, ("shard", "ctx")),
        P(None, ("shard", "ctx")),
        P(("shard", "ctx"), None),
        P(None, ("shard", "ctx")),
        P(None, ("shard", "ctx")),
        P(("shard", "ctx"), None),
        P(("shard", "ctx")),
    )
    out_specs = (
        P(("rep", "shard"), "ctx", None),
        P(("rep", "shard"), "ctx", None),
        P(None, ("shard", "ctx")),
        P(None, ("shard", "ctx")),
        P(None, ("shard", "ctx")),
        P(("shard", "ctx"), None),
        P(None, ("shard", "ctx")),
        P(None, ("shard", "ctx")),
        P(("shard", "ctx"), None),
        P(("shard", "ctx")),
    )
    return jax.shard_map(any_body, mesh=mesh, in_specs=in_specs, out_specs=out_specs, check_vma=False)
```

```python
import functools
import math

import jax
import jax.numpy as jnp
from jax import lax
from jax.experimental import pallas as pl
from jax.experimental.pallas import tpu as pltpu
from jax.sharding import PartitionSpec as P

QUERY_HEADS = 16
KEY_VALUE_HEADS = 8
HEAD_DIM = 128

MESH = pl.DeviceIdType.MESH

EPSILON = 1e-06
ROPE_BASE = 1000000.0


def rms_scale(values_in):
    return lax.rsqrt(jnp.mean(values_in * values_in, axis=-1, keepdims=True) + EPSILON)


def norm_backward(grad_in, values_in, scale_in, gain_in):
    grad_norm = grad_in * gain_in
    unit = values_in * scale_in
    return scale_in * (grad_norm - unit * jnp.mean(grad_norm * unit, axis=-1, keepdims=True))


def rope_tables(position_ids):
    half_dim = HEAD_DIM // 2
    inverse = 1.0 / ROPE_BASE ** (jnp.arange(half_dim, dtype=jnp.float32) * (2.0 / HEAD_DIM))
    angle = position_ids.astype(jnp.float32)[..., None] * inverse
    return (jnp.cos(angle)[:, :, None, :], jnp.sin(angle)[:, :, None, :])


def rotate(values_in, cosine, sine):
    half_dim = values_in.shape[-1] // 2
    first = values_in[..., :half_dim]
    second = values_in[..., half_dim:]
    return jnp.concatenate(
        [first * cosine - second * sine, second * cosine + first * sine], axis=-1
    )


def rotate_back(grad_in, cosine, sine):
    half_dim = grad_in.shape[-1] // 2
    first = grad_in[..., :half_dim]
    second = grad_in[..., half_dim:]
    return jnp.concatenate(
        [first * cosine + second * sine, second * cosine - first * sine], axis=-1
    )


def float_product(left, right):
    return jnp.dot(left, right, preferred_element_type=jnp.float32)


def against_rows(left, right):
    return lax.dot_general(
        left, right, (((1,), (1,)), ((), ())), preferred_element_type=jnp.float32
    )


def over_tokens(left, right):
    return lax.dot_general(
        left, right, (((0,), (0,)), ((), ())), preferred_element_type=jnp.float32
    )


def body(
    tokens,
    positions,
    segments,
    cotangent,
    w_query,
    key_weight,
    value_weight,
    output_weight,
    w_gate,
    w_up,
    w_down,
    norm_gains,
):
    sequence_count, local_length, model_width = tokens.shape
    total_rows = sequence_count * local_length
    group_width = QUERY_HEADS // KEY_VALUE_HEADS
    score_scale = 1.0 / math.sqrt(HEAD_DIM)
    local_start = lax.axis_index("ctx") * local_length
    local_pos = lax.dynamic_slice_in_dim(positions, local_start, local_length, 1)
    local_seg = lax.dynamic_slice_in_dim(segments, local_start, local_length, 1)
    wq_full, full_key_weight, full_value_weight, wo_full, gains_full = (
        lax.all_gather(w_query, ("shard", "ctx"), axis=1, tiled=True),
        lax.all_gather(key_weight, ("shard", "ctx"), axis=1, tiled=True),
        lax.all_gather(value_weight, ("shard", "ctx"), axis=1, tiled=True),
        lax.all_gather(output_weight, ("shard", "ctx"), axis=0, tiled=True),
        lax.all_gather(norm_gains, ("shard", "ctx"), axis=0, tiled=True),
    )
    gain_all = gains_full.astype(jnp.float32)
    g_attn = gain_all[:model_width]
    g_query = gain_all[model_width : model_width + HEAD_DIM]
    key_gain = gain_all[model_width + HEAD_DIM : model_width + 2 * HEAD_DIM]
    g_mlp = gain_all[model_width + 2 * HEAD_DIM :]
    x_rows = tokens.reshape(total_rows, model_width).astype(jnp.float32)
    scale_in = rms_scale(x_rows)
    normed_input = (x_rows * scale_in * g_attn).astype(jnp.bfloat16)
    query = float_product(normed_input, wq_full).reshape(
        sequence_count, local_length, QUERY_HEADS, HEAD_DIM
    )
    key_rows = float_product(normed_input, full_key_weight).reshape(
        sequence_count, local_length, KEY_VALUE_HEADS, HEAD_DIM
    )
    value_rows = (
        float_product(normed_input, full_value_weight)
        .astype(jnp.bfloat16)
        .reshape(sequence_count, local_length, KEY_VALUE_HEADS, HEAD_DIM)
    )
    q_scale = rms_scale(query)
    key_scale = rms_scale(key_rows)
    cosine, sine = rope_tables(local_pos)
    query_rotated = rotate(query * q_scale * g_query, cosine, sine).astype(jnp.bfloat16)
    k_rot = rotate(key_rows * key_scale * key_gain, cosine, sine).astype(jnp.bfloat16)
    keys_all, values_all = (
        lax.all_gather(k_rot, "ctx", axis=1, tiled=True),
        lax.all_gather(value_rows, "ctx", axis=1, tiled=True),
    )
    allowed = (
        (local_seg[:, :, None] == segments[:, None, :])
        & (positions[:, None, :] <= local_pos[:, :, None])
    )[:, None, None]
    query_group = query_rotated.reshape(
        sequence_count, local_length, KEY_VALUE_HEADS, group_width, HEAD_DIM
    )
    scores = (
        jnp.einsum("bqkgd,bskd->bkgqs", query_group, keys_all, preferred_element_type=jnp.float32)
        * score_scale
    )
    exponent = jnp.where(allowed, jnp.exp(scores), 0.0)
    denominator = jnp.sum(exponent, axis=-1)
    log_total = jnp.log(denominator)
    probs = (exponent / denominator[..., None]).astype(jnp.bfloat16)
    attention_output = jnp.einsum(
        "bkgqs,bskd->bqkgd", probs, values_all, preferred_element_type=jnp.float32
    )
    attention_output = attention_output.astype(jnp.bfloat16).reshape(
        total_rows, QUERY_HEADS * HEAD_DIM
    )
    mixed_in = x_rows + float_product(attention_output, wo_full)
    scale_mid = rms_scale(mixed_in)
    normed_mid = (mixed_in * scale_mid * g_mlp).astype(jnp.bfloat16)
    wg_full, wu_full, wd_full = (
        lax.all_gather(w_gate, ("shard", "ctx"), axis=1, tiled=True),
        lax.all_gather(w_up, ("shard", "ctx"), axis=1, tiled=True),
        lax.all_gather(w_down, ("shard", "ctx"), axis=0, tiled=True),
    )
    gate_pre = float_product(normed_mid, wg_full)
    up_pre = float_product(normed_mid, wu_full)
    sigmoid_gate = jax.nn.sigmoid(gate_pre)
    hidden = (gate_pre * sigmoid_gate * up_pre).astype(jnp.bfloat16)
    block_sum = mixed_in + float_product(hidden, wd_full)
    block_out = block_sum.astype(jnp.bfloat16).reshape(sequence_count, local_length, model_width)
    grad_rows = cotangent.reshape(total_rows, model_width)
    d_hidden = against_rows(grad_rows, wd_full)
    grad_down = over_tokens(hidden, grad_rows)
    d_gate = (d_hidden * up_pre * sigmoid_gate * (1.0 + gate_pre * (1.0 - sigmoid_gate))).astype(
        jnp.bfloat16
    )
    d_up = (d_hidden * gate_pre * sigmoid_gate).astype(jnp.bfloat16)
    grad_gate = over_tokens(normed_mid, d_gate)
    grad_up = over_tokens(normed_mid, d_up)
    owned_gate, owned_up, owned_down = (
        lax.psum_scatter(grad_gate, ("shard", "ctx"), scatter_dimension=1, tiled=True),
        lax.psum_scatter(grad_up, ("shard", "ctx"), scatter_dimension=1, tiled=True),
        lax.psum_scatter(grad_down, ("shard", "ctx"), scatter_dimension=0, tiled=True),
    )
    total_gate, total_up, total_down = (
        lax.psum(owned_gate.astype(jnp.bfloat16), "rep").astype(jnp.float32),
        lax.psum(owned_up.astype(jnp.bfloat16), "rep").astype(jnp.float32),
        lax.psum(owned_down.astype(jnp.bfloat16), "rep").astype(jnp.float32),
    )
    d_mid = against_rows(d_gate, wg_full) + against_rows(d_up, wu_full)
    dg_mlp = jnp.sum(d_mid * mixed_in * scale_mid, axis=0)
    d_resid = grad_rows.astype(jnp.float32) + norm_backward(d_mid, mixed_in, scale_mid, g_mlp)
    residual_gradient_bfloat = d_resid.astype(jnp.bfloat16)
    grad_output = over_tokens(attention_output, residual_gradient_bfloat)
    attention_gradient = (
        against_rows(residual_gradient_bfloat, wo_full)
        .astype(jnp.bfloat16)
        .reshape(sequence_count, local_length, KEY_VALUE_HEADS, group_width, HEAD_DIM)
    )
    attention_heads = attention_output.reshape(
        sequence_count, local_length, KEY_VALUE_HEADS, group_width, HEAD_DIM
    )
    row_delta = jnp.sum(
        attention_gradient.astype(jnp.float32) * attention_heads.astype(jnp.float32), axis=-1
    )
    row_delta = jnp.transpose(row_delta, (0, 2, 3, 1))
    scores_again = (
        jnp.einsum("bqkgd,bskd->bkgqs", query_group, keys_all, preferred_element_type=jnp.float32)
        * score_scale
    )
    probs_back = jnp.where(allowed, jnp.exp(scores_again - log_total[..., None]), 0.0)
    probs_round = probs_back.astype(jnp.bfloat16)
    values_gradient = jnp.einsum(
        "bkgqs,bqkgd->bskd", probs_round, attention_gradient, preferred_element_type=jnp.float32
    )
    d_probs = jnp.einsum(
        "bqkgd,bskd->bkgqs", attention_gradient, values_all, preferred_element_type=jnp.float32
    )
    d_scores = (probs_back * (d_probs - row_delta[..., None])).astype(jnp.bfloat16)
    d_qrot = (
        jnp.einsum("bkgqs,bskd->bqkgd", d_scores, keys_all, preferred_element_type=jnp.float32)
        * score_scale
    )
    d_krot = (
        jnp.einsum("bkgqs,bqkgd->bskd", d_scores, query_group, preferred_element_type=jnp.float32)
        * score_scale
    )
    d_keys, value_rows_gradient = (
        lax.psum_scatter(
            d_krot.astype(jnp.bfloat16), "ctx", scatter_dimension=1, tiled=True
        ).astype(jnp.float32),
        lax.psum_scatter(
            values_gradient.astype(jnp.bfloat16), "ctx", scatter_dimension=1, tiled=True
        ).astype(jnp.float32),
    )
    d_qn = rotate_back(
        d_qrot.reshape(sequence_count, local_length, QUERY_HEADS, HEAD_DIM), cosine, sine
    )
    normed_key_gradient = rotate_back(d_keys, cosine, sine)
    dg_query = jnp.sum(d_qn * query * q_scale, axis=(0, 1, 2))
    dg_key = jnp.sum(normed_key_gradient * key_rows * key_scale, axis=(0, 1, 2))
    d_query = (
        norm_backward(d_qn, query, q_scale, g_query)
        .astype(jnp.bfloat16)
        .reshape(total_rows, QUERY_HEADS * HEAD_DIM)
    )
    key_gradient = (
        norm_backward(normed_key_gradient, key_rows, key_scale, key_gain)
        .astype(jnp.bfloat16)
        .reshape(total_rows, KEY_VALUE_HEADS * HEAD_DIM)
    )
    value_gradient = value_rows_gradient.astype(jnp.bfloat16).reshape(
        total_rows, KEY_VALUE_HEADS * HEAD_DIM
    )
    grad_query = over_tokens(normed_input, d_query)
    grad_key = over_tokens(normed_input, key_gradient)
    grad_value = over_tokens(normed_input, value_gradient)
    d_in = (
        against_rows(d_query, wq_full)
        + against_rows(key_gradient, full_key_weight)
        + against_rows(value_gradient, full_value_weight)
    )
    dg_attn = jnp.sum(d_in * x_rows * scale_in, axis=0)
    grad_input = (d_resid + norm_backward(d_in, x_rows, scale_in, g_attn)).reshape(
        sequence_count, local_length, model_width
    )
    grad_gains = jnp.concatenate([dg_attn, dg_query, dg_key, dg_mlp])
    owned_query, owned_key, owned_value, owned_output, owned_gains = (
        lax.psum_scatter(grad_query, ("shard", "ctx"), scatter_dimension=1, tiled=True),
        lax.psum_scatter(grad_key, ("shard", "ctx"), scatter_dimension=1, tiled=True),
        lax.psum_scatter(grad_value, ("shard", "ctx"), scatter_dimension=1, tiled=True),
        lax.psum_scatter(grad_output, ("shard", "ctx"), scatter_dimension=0, tiled=True),
        lax.psum_scatter(grad_gains, ("shard", "ctx"), scatter_dimension=0, tiled=True),
    )
    total_query, total_key, total_value, total_output, total_gains = (
        lax.psum(owned_query.astype(jnp.bfloat16), "rep").astype(jnp.float32),
        lax.psum(owned_key.astype(jnp.bfloat16), "rep").astype(jnp.float32),
        lax.psum(owned_value.astype(jnp.bfloat16), "rep").astype(jnp.float32),
        lax.psum(owned_output.astype(jnp.bfloat16), "rep").astype(jnp.float32),
        lax.psum(owned_gains.astype(jnp.bfloat16), "rep").astype(jnp.float32),
    )
    return (
        block_out,
        grad_input,
        total_query,
        total_key,
        total_value,
        total_output,
        total_gate,
        total_up,
        total_down,
        total_gains,
    )


def row_plan(head_half, ff):
    sizes = (
        ("q", HEAD_DIM, HEAD_DIM),
        ("k", head_half, HEAD_DIM),
        ("v", head_half, HEAD_DIM),
        ("o", HEAD_DIM, HEAD_DIM),
        ("g", ff, ff),
        ("u", ff, ff),
        ("d", ff, ff),
    )
    plan, own, full = {}, 0, 0
    for name, own_rows, block_rows in sizes:
        plan[name] = (own, own_rows, full, block_rows)
        own, full = own + own_rows, full + 4 * block_rows
    return plan, own, full


def plain(left, right):
    return lax.dot_general(left, right, (((1,), (0,)), ((), ())), preferred_element_type=jnp.float32)


def swap_halves(values_in):
    return pltpu.roll(values_in, values_in.shape[-1] // 2, 1)


def rows(start, size, step):
    return pl.ds(pl.multiple_of(start, step), size)


def hand_over(*refs):
    count = len(refs) // 2
    for src, dst in zip(refs[:count], refs[count:]):
        dst[...] = src[...]


def layer_kernel(
    plan,
    tok,
    cot,
    w_q,
    k_rows,
    v_rows,
    out_rows,
    gate_rows,
    up_rows,
    down_rows,
    gain_in,
    pos,
    seg,
    cosine,
    sine,
    block_out,
    grad_in,
    grad_q,
    grad_k,
    grad_v,
    grad_o,
    grad_g,
    grad_u,
    grad_d,
    gain_out,
    x_all,
    c_all,
    nx,
    nm,
    res,
    own_mid,
    own_res,
    wb,
    qf,
    kf,
    qr,
    kr,
    vb,
    prob,
    att,
    hid,
    dga,
    dup,
    dqb,
    dkb,
    dvb,
    mixed,
    dres,
    part_a,
    part_b,
    got_a,
    got_b,
    got_c,
    got_d,
    gz,
    gsum,
    gz_s,
    gfull,
    dgt,
    dz,
    dsum,
    dz_s,
    dtot,
    dz_x,
    gb,
    rk,
    hs,
    ry,
    kvh,
    kvr,
    xo,
    rx,
    send_sem,
    recv_sem,
):
    sequences, span, width = tok.shape
    ctx = lax.axis_size("ctx")
    length = span * ctx
    heads = 4
    scale = 1.0 / math.sqrt(HEAD_DIM)
    r, s, c = lax.axis_index("rep"), lax.axis_index("shard"), lax.axis_index("ctx")
    core, side = s % 2, s // 2
    sib, opp = s + 1 - 2 * core, (s + 2) % 4
    dia = (sib + 2) % 4
    mine, theirs = core * 2 + side, core * 2 + 1 - side
    half = c % 2
    near = c + 1 - 2 * half
    far = (c + 2) % 4
    other = (near + 2) % 4
    both = range(sequences)
    sends, lent, returned = [], [], []

    def send(src, dst, **where):
        at = len(sends)
        copy = pltpu.make_async_remote_copy(
            src_ref=src,
            dst_ref=dst,
            send_sem=send_sem.at[at],
            recv_sem=recv_sem.at[at],
            device_id=where,
            device_id_type=MESH,
        )
        copy.start()
        sends.append(copy)
        return copy

    def arrive(copies):
        for copy in copies:
            copy.wait_recv()

    def reclaim(copies):
        for copy in copies:
            copy.wait_send()
            returned.append(copy)

    def gather_start(src, dst, b):
        dst[b, c] = src[b]
        across = send(src.at[b], dst.at[b, c], ctx=far)
        beside = send(src.at[b], dst.at[b, c], ctx=near)
        return beside, across

    def gather_pass(dst, b, pair):
        arrive([pair[1]])
        return pair[0], send(dst.at[b, far], dst.at[b, far], ctx=near)

    def reduce_start(src, got, b):
        first = send(src.at[other, b], got.at[0, b], ctx=near)
        second = send(src.at[near, b], got.at[1, b], ctx=near)
        lent.extend((first, second))
        return first, second

    def reduce_pass(src, got, b, pair):
        arrive([pair[0]])
        total = src[far, b].astype(jnp.float32) + got[0, b].astype(jnp.float32)
        src[far, b] = total.astype(jnp.bfloat16)
        third = send(src.at[far, b], got.at[2, b], ctx=far)
        lent.append(third)
        return pair[1], third

    def reduce_end(src, got, b, pair):
        arrive(pair)
        total = src[c, b].astype(jnp.float32) + got[1, b].astype(jnp.float32)
        return total + got[2, b].astype(jnp.float32)

    def block(name, at):
        _, _, off, size = plan[name]
        return rows(off + at * size, size, 64)

    def spread_rows(own):
        there = send(wb.at[own], wb.at[own], shard=opp)
        return [there], [send(wb.at[own], wb.at[own], shard=sib)]

    def spread(name):
        return spread_rows(block(name, mine))

    def pass_on(name):
        got = block(name, theirs)
        return send(wb.at[got], wb.at[got], shard=sib)

    def own_rows(name):
        off, size = plan[name][:2]
        return pl.ds(off, size)

    def matrix(name):
        _, _, off, size = plan[name]
        return wb[pl.ds(off, 4 * size), :]

    def whole(ref, b):
        return ref[b].reshape(length, width)

    def split(values_in, dst, b):
        for j in range(ctx):
            dst[j, b] = values_in[j * span : (j + 1) * span].astype(jnp.bfloat16)

    barrier = pltpu.get_barrier_semaphore()
    peers = [{"ctx": near}, {"ctx": far}, {"ctx": other}]
    peers += [{"shard": sib}, {"shard": opp}, {"shard": dia}, {"rep": 1 - r}]
    for peer in peers:
        pl.semaphore_signal(barrier, inc=1, device_id=peer, device_id_type=MESH)
    pl.semaphore_wait(barrier, len(peers))

    head_half = plan["k"][1]
    gains = [send(gain_in, gz.at[i], ctx=p) for i, p in enumerate((near, far, other))]
    kv_in, spreads = [], {}
    for n, src in zip("kv", (k_rows, v_rows)):
        first = plan[n][2] + mine * HEAD_DIM
        at = rows(first + half * head_half, head_half, 64)
        wb[at, :] = src[...]
        kv_in.append(send(wb.at[at], wb.at[at], ctx=near))
        spreads[n] = spread_rows(at)
    tok_in = [gather_start(tok, x_all, b) for b in both]
    wb[block("q", mine), :] = w_q[...].astype(jnp.float32).T.astype(jnp.bfloat16)
    for n, src in zip("ogud", (out_rows, gate_rows, up_rows, down_rows)):
        wb[block(n, mine), :] = src[...]
    arrive(gains)
    gsum[...] = gain_in[...] + gz[0] + gz[1] + gz[2]
    gains = [send(gsum, gz_s.at[i], shard=p) for i, p in enumerate((sib, opp, dia))]
    spreads["q"] = spread("q")
    arrive(kv_in)
    for n in "kv":
        first = plan[n][2] + mine * HEAD_DIM
        late = spread_rows(rows(first + (1 - half) * head_half, head_half, 64))
        for early, more in zip(spreads[n], late):
            early.extend(more)
    spreads["o"] = spread("o")
    arrive(gains)
    gfull[...] = gsum[...] + gz_s[0] + gz_s[1] + gz_s[2]
    g_attn = gfull[0:1, :]
    g_mlp = gfull[1:2, :]
    g_query = gfull[2:3, :HEAD_DIM]
    g_key = gfull[2:3, HEAD_DIM : 2 * HEAD_DIM]
    passed = {}

    def pass_weights(names):
        for n in names:
            arrive(spreads[n][0])
            passed[n] = pass_on(n)

    def have_weights(names):
        for n in names:
            arrive(spreads[n][1] + [passed[n]])

    tok_in[0] = gather_pass(x_all, 0, tok_in[0])
    pass_weights("qkv")
    tok_in[1] = gather_pass(x_all, 1, tok_in[1])
    cot_in = [gather_start(cot, c_all, 0)]

    def norm_rows(b):
        def one(j, carry):
            x = x_all[b, j].astype(jnp.float32)
            nx[b, j] = (x * rms_scale(x) * g_attn).astype(jnp.bfloat16)
            return carry

        lax.fori_loop(0, ctx, one, 0)

    def attend(b):
        x = whole(nx, b)
        query = against_rows(x, matrix("q"))
        key = against_rows(x, matrix("k"))
        value = against_rows(x, matrix("v")).astype(jnp.bfloat16)
        cos_b, sin_b = cosine[b], sine[b]
        key_at = jnp.broadcast_to(pos[b : b + 1, :].astype(jnp.float32), (length, length))
        key_doc = jnp.broadcast_to(seg[b : b + 1, :].astype(jnp.float32), (length, length))
        allowed = (key_doc.T == key_doc) & (key_at <= key_at.T)
        for h in range(heads):
            at = slice(h * HEAD_DIM, (h + 1) * HEAD_DIM)
            q, k, v = query[:, at], key[:, at], value[:, at]
            qn = q * rms_scale(q) * g_query
            kn = k * rms_scale(k) * g_key
            q_rot = (qn * cos_b + swap_halves(qn) * sin_b).astype(jnp.bfloat16)
            k_rot = (kn * cos_b + swap_halves(kn) * sin_b).astype(jnp.bfloat16)
            qf[b, h], kf[b, h] = q, k
            qr[b, h], kr[b, h], vb[b, h] = q_rot, k_rot, v
            scores = against_rows(q_rot, k_rot) * scale
            exponent = jnp.where(allowed, jnp.exp(scores), 0.0)
            p = exponent / jnp.sum(exponent, axis=-1, keepdims=True)
            prob[b, h] = p
            att[b, :, at] = plain(p.astype(jnp.bfloat16), v).astype(jnp.bfloat16)

    out_part = []
    for b in both:
        arrive(tok_in[b])
        norm_rows(b)
        if b == 0:
            have_weights("qkv")
        else:
            for n in "gud":
                spreads[n] = spread(n)
        attend(b)
        if b == 0:
            pass_weights("o")
            have_weights("o")
        else:
            out_part[0] = reduce_pass(part_a, got_a, 0, out_part[0])
        split(plain(att[b], matrix("o")), part_a, b)
        out_part.append(reduce_start(part_a, got_a, b))
        if b == 0:
            cot_in.append(gather_start(cot, c_all, 1))
    out_part[1] = reduce_pass(part_a, got_a, 1, out_part[1])
    first_parts = list(lent)
    mid_in = []
    for b in both:
        m = tok[b].astype(jnp.float32) + reduce_end(part_a, got_a, b, out_part[b])
        mixed[b] = m
        own_mid[b] = (m * rms_scale(m) * g_mlp).astype(jnp.bfloat16)
        mid_in.append(gather_start(own_mid, nm, b))
        cot_in[b] = gather_pass(c_all, b, cot_in[b])
    pass_weights("gud")
    mid_in = [gather_pass(nm, b, mid_in[b]) for b in both]
    have_weights("gud")

    def feed(b):
        n, ct = whole(nm, b), whole(c_all, b)
        gate = against_rows(n, matrix("g"))
        up = against_rows(n, matrix("u"))
        d_hidden = against_rows(ct, matrix("d"))
        sig = jax.nn.sigmoid(gate)
        hid[b] = (gate * sig * up).astype(jnp.bfloat16)
        d_gate = (d_hidden * up * sig * (1.0 + gate * (1.0 - sig))).astype(jnp.bfloat16)
        d_up = (d_hidden * gate * sig).astype(jnp.bfloat16)
        dga[b], dup[b] = d_gate, d_up
        split(plain(d_gate, matrix("g")) + plain(d_up, matrix("u")), part_b, b)

    mid_back = []
    for b in both:
        arrive(cot_in[b])
        arrive(mid_in[b])
        feed(b)
        mid_back.append(reduce_start(part_b, got_b, b))

    def weigh(name, left, right):
        _, _, off, size = plan[name]
        right = right[...].reshape(sequences * length, width)
        chunk = 256

        def some(i, carry):
            at = pl.multiple_of(i * chunk, chunk)
            lhs = left[:, :, pl.ds(at, chunk)].reshape(sequences * length, chunk)
            gb[rows(off + at, chunk, 64), :] = over_tokens(lhs, right).astype(jnp.bfloat16)
            return carry

        lax.fori_loop(0, 4 * size // chunk, some, 0)
        return send(
            gb.at[rows(off + (1 - core) * 2 * size, 2 * size, 64)],
            rk.at[pl.ds(off // 2, 2 * size)],
            shard=sib,
        )

    def core_sum(name, at):
        _, _, off, size = plan[name]
        here = gb[rows(off + (core * 2 + at) * size, size, 64), :]
        there = rk[rows(off // 2 + at * size, size, 64), :]
        return here.astype(jnp.float32) + there.astype(jnp.float32)

    def drain_core(name, copy):
        _, _, off, size = plan[name]
        arrive([copy])
        at = pl.ds(off // 4, size)
        hs[at, :] = core_sum(name, 1 - side).astype(jnp.bfloat16)
        return send(hs.at[at], ry.at[at], shard=opp)

    def drain_side(name, copy):
        own, own_size, off, size = plan[name]
        arrive([copy])
        total = core_sum(name, side) + ry[pl.ds(off // 4, size), :].astype(jnp.float32)
        total = total.astype(jnp.bfloat16)
        at = pl.ds(own, own_size)
        if own_size == size:
            xo[at, :] = total
            return send(xo.at[at], rx.at[at], rep=1 - r)
        i = "kv".index(name)
        kvh[i] = total
        return send(kvh.at[i, rows((1 - half) * own_size, own_size, 64)], kvr.at[i], ctx=near)

    def drain_pair(name, copy):
        own, own_size, _, _ = plan[name]
        arrive([copy])
        i = "kv".index(name)
        total = kvh[i, rows(half * own_size, own_size, 64), :].astype(jnp.float32)
        at = pl.ds(own, own_size)
        xo[at, :] = (total + kvr[i].astype(jnp.float32)).astype(jnp.bfloat16)
        return send(xo.at[at], rx.at[at], rep=1 - r)

    results = dict(zip("qkvogud", (grad_q, grad_k, grad_v, grad_o, grad_g, grad_u, grad_d)))

    def drain_rep(name, copy):
        at = own_rows(name)
        arrive([copy])
        total = xo[at, :].astype(jnp.float32) + rx[at, :].astype(jnp.float32)
        out = results[name]
        out[...] = total.T if name == "q" else total

    dgt[...] = jnp.zeros_like(dgt)
    res_in = []

    def enter(b):
        d_mid = reduce_end(part_b, got_b, b, mid_back[b])
        m = mixed[b]
        r_mid = rms_scale(m)
        dgt[1:2, :] += jnp.sum(d_mid * m * r_mid, axis=0, keepdims=True)
        d_resid = cot[b].astype(jnp.float32) + norm_backward(d_mid, m, r_mid, g_mlp)
        dres[b] = d_resid
        own_res[b] = d_resid.astype(jnp.bfloat16)
        res_in.append(gather_start(own_res, res, b))

    reclaim(first_parts)
    moving = {}
    moving["d"] = weigh("d", hid, c_all)
    moving["g"] = weigh("g", dga, nm)
    moving["d"] = drain_core("d", moving["d"])
    mid_back[0] = reduce_pass(part_b, got_b, 0, mid_back[0])
    moving["u"] = weigh("u", dup, nm)
    moving["g"] = drain_core("g", moving["g"])
    mid_back[1] = reduce_pass(part_b, got_b, 1, mid_back[1])
    second_parts = lent[len(first_parts) :]
    enter(0)
    moving["u"] = drain_core("u", moving["u"])
    enter(1)
    moving["d"] = drain_side("d", moving["d"])
    for b in both:
        split(plain(hid[b], matrix("d")), part_a, b)
    res_in = [gather_pass(res, b, res_in[b]) for b in both]
    out_back = [reduce_start(part_a, got_c, b) for b in both]
    reclaim(second_parts)

    def attend_back(b):
        d_att = against_rows(whole(res, b), matrix("o")).astype(jnp.bfloat16)
        cos_b, sin_b = cosine[b], sine[b]

        def through(d_rot, u, gain):
            d_n = d_rot * cos_b - swap_halves(d_rot) * sin_b
            u_scale = rms_scale(u)
            gain_row = jnp.sum(d_n * u * u_scale, axis=0, keepdims=True)
            return norm_backward(d_n, u, u_scale, gain).astype(jnp.bfloat16), gain_row

        for h in range(heads):
            at = slice(h * HEAD_DIM, (h + 1) * HEAD_DIM)
            da, p = d_att[:, at], prob[b, h]
            delta = jnp.sum(
                da.astype(jnp.float32) * att[b, :, at].astype(jnp.float32), axis=-1, keepdims=True
            )
            dvb[b, :, at] = over_tokens(p.astype(jnp.bfloat16), da).astype(jnp.bfloat16)
            d_p = against_rows(da, vb[b, h])
            d_s = (p * (d_p - delta)).astype(jnp.bfloat16)
            d_q, row_q = through(plain(d_s, kr[b, h]) * scale, qf[b, h], g_query)
            d_k, row_k = through(over_tokens(d_s, qr[b, h]) * scale, kf[b, h], g_key)
            dqb[b, :, at] = d_q
            dkb[b, :, at] = d_k
            dgt[2:3, :HEAD_DIM] += row_q
            dgt[2:3, HEAD_DIM : 2 * HEAD_DIM] += row_k
        d_in = plain(dqb[b], matrix("q")) + plain(dkb[b], matrix("k")) + plain(dvb[b], matrix("v"))
        split(d_in, part_b, b)

    arrive(res_in[0])
    moving["g"] = drain_side("g", moving["g"])
    attend_back(0)
    in_back = [reduce_start(part_b, got_d, 0)]
    out_back[0] = reduce_pass(part_a, got_c, 0, out_back[0])
    arrive(res_in[1])
    moving["o"] = weigh("o", att, res)
    moving["u"] = drain_side("u", moving["u"])
    moving["o"] = drain_core("o", moving["o"])
    attend_back(1)
    in_back.append(reduce_start(part_b, got_d, 1))
    out_back[1] = reduce_pass(part_a, got_c, 1, out_back[1])
    moving["k"] = weigh("k", dkb, nx)
    moving["v"] = weigh("v", dvb, nx)
    moving["k"] = drain_core("k", moving["k"])
    in_back[0] = reduce_pass(part_b, got_d, 0, in_back[0])
    moving["q"] = weigh("q", dqb, nx)
    moving["v"] = drain_core("v", moving["v"])
    moving["o"] = drain_side("o", moving["o"])
    moving["q"] = drain_core("q", moving["q"])
    in_back[1] = reduce_pass(part_b, got_d, 1, in_back[1])
    moving["k"] = drain_side("k", moving["k"])
    moving["v"] = drain_side("v", moving["v"])
    moving["q"] = drain_side("q", moving["q"])
    drain_rep("d", moving["d"])
    drain_rep("g", moving["g"])
    for b in both:
        d_in = reduce_end(part_b, got_d, b, in_back[b])
        x = tok[b].astype(jnp.float32)
        r_in = rms_scale(x)
        dgt[0:1, :] += jnp.sum(d_in * x * r_in, axis=0, keepdims=True)
        grad_in[b] = dres[b] + norm_backward(d_in, x, r_in, g_attn)
    gains = [send(dgt, dz.at[i], ctx=p) for i, p in enumerate((near, far, other))]
    moving["k"] = drain_pair("k", moving["k"])
    moving["v"] = drain_pair("v", moving["v"])
    arrive(gains)
    dsum[...] = dgt[...] + dz[0] + dz[1] + dz[2]
    gains = [send(dsum, dz_s.at[i], shard=p) for i, p in enumerate((sib, opp, dia))]
    drain_rep("u", moving["u"])
    arrive(gains)
    dtot[...] = dsum[...] + dz_s[0] + dz_s[1] + dz_s[2]
    gains = [send(dtot, dz_x, rep=1 - r)]
    for b in both:
        total = mixed[b] + reduce_end(part_a, got_c, b, out_back[b])
        block_out[b] = total.astype(jnp.bfloat16)
    for n in "oqkv":
        drain_rep(n, moving[n])
    arrive(gains)
    gain_out[...] = dtot[...] + dz_x[...]
    for copy in sends:
        if not any(copy is late for late in returned):
            copy.wait_send()


def whole_layer_body(
    tokens,
    positions,
    segments,
    cotangent,
    w_query,
    key_weight,
    value_weight,
    output_weight,
    w_gate,
    w_up,
    w_down,
    norm_gains,
):
    sequences, span, width = tokens.shape
    ctx = lax.axis_size("ctx")
    length = span * ctx
    ff = w_gate.shape[1]
    half = key_weight.shape[1]
    plan, own_total, full_total = row_plan(half, ff)
    heads = 4
    k_rows, v_rows, g_rows, u_rows = key_weight.T, value_weight.T, w_gate.T, w_up.T
    count = norm_gains.shape[0]
    place = lax.axis_index("shard") * ctx + lax.axis_index("ctx")
    all_gains = width * 2 + 2 * HEAD_DIM
    spread_gains = lax.dynamic_update_slice(
        jnp.zeros((all_gains,), jnp.float32), norm_gains.astype(jnp.float32), (place * count,)
    )
    gain_rows = jnp.concatenate(
        [
            spread_gains[:width],
            spread_gains[width + 2 * HEAD_DIM :],
            spread_gains[width : width + 2 * HEAD_DIM],
            jnp.zeros((6 * width - 2 * HEAD_DIM,), jnp.float32),
        ]
    ).reshape(8, width)
    lane = jnp.arange(HEAD_DIM)
    power = (lane % (HEAD_DIM // 2)).astype(jnp.float32) * (2.0 / HEAD_DIM)
    angle = positions.astype(jnp.float32)[..., None] * (1.0 / ROPE_BASE**power)
    cosine = jnp.cos(angle)
    sine = jnp.where(lane < HEAD_DIM // 2, -1.0, 1.0) * jnp.sin(angle)

    bf, f32 = jnp.bfloat16, jnp.float32
    gathered = pltpu.VMEM((sequences, ctx, span, width), bf)
    own_block = pltpu.VMEM((sequences, span, width), bf)
    own_float = pltpu.VMEM((sequences, span, width), f32)
    head_float = pltpu.VMEM((sequences, heads, length, HEAD_DIM), f32)
    head_half = pltpu.VMEM((sequences, heads, length, HEAD_DIM), bf)
    head_lanes = pltpu.VMEM((sequences, length, heads * HEAD_DIM), bf)
    ff_lanes = pltpu.VMEM((sequences, length, heads * ff), bf)
    parts = pltpu.VMEM((ctx, sequences, span, width), bf)
    got = pltpu.VMEM((3, sequences, span, width), bf)
    tile = pltpu.VMEM((8, width), f32)
    tiles_c = pltpu.VMEM((ctx - 1, 8, width), f32)
    tiles_s = pltpu.VMEM((3, 8, width), f32)

    def row_buffer(n):
        return pltpu.VMEM((n, width), bf)

    copies = 128
    vmem = pl.BlockSpec(memory_space=pltpu.VMEM)
    outs = pl.pallas_call(
        functools.partial(layer_kernel, plan),
        out_shape=(
            jax.ShapeDtypeStruct(tokens.shape, bf),
            jax.ShapeDtypeStruct(tokens.shape, f32),
            *(
                jax.ShapeDtypeStruct(weight.shape, f32)
                for weight in (
                    w_query,
                    k_rows,
                    v_rows,
                    output_weight,
                    g_rows,
                    u_rows,
                    w_down,
                )
            ),
            jax.ShapeDtypeStruct((8, width), f32),
        ),
        in_specs=[vmem] * 14,
        out_specs=[vmem] * 10,
        scratch_shapes=[
            gathered,
            gathered,
            gathered,
            gathered,
            gathered,
            own_block,
            own_block,
            row_buffer(full_total),
            head_float,
            head_float,
            head_half,
            head_half,
            head_half,
            pltpu.VMEM((sequences, heads, length, length), f32),
            head_lanes,
            ff_lanes,
            ff_lanes,
            ff_lanes,
            head_lanes,
            head_lanes,
            head_lanes,
            own_float,
            own_float,
            parts,
            parts,
            got,
            got,
            got,
            got,
            tiles_c,
            tile,
            tiles_s,
            tile,
            tile,
            tiles_c,
            tile,
            tiles_s,
            tile,
            tile,
            row_buffer(full_total),
            row_buffer(full_total // 2),
            row_buffer(full_total // 4),
            row_buffer(full_total // 4),
            pltpu.VMEM((2, HEAD_DIM, width), bf),
            pltpu.VMEM((2, half, width), bf),
            row_buffer(own_total),
            row_buffer(own_total),
            pltpu.SemaphoreType.DMA((copies,)),
            pltpu.SemaphoreType.DMA((copies,)),
        ],
        compiler_params=pltpu.CompilerParams(
            collective_id=0, has_side_effects=True, vmem_limit_bytes=67043328
        ),
    )(
        tokens,
        cotangent,
        w_query,
        k_rows,
        v_rows,
        output_weight,
        g_rows,
        u_rows,
        w_down,
        gain_rows,
        positions,
        segments,
        cosine,
        sine,
    )
    outs = pl.pallas_call(
        hand_over,
        out_shape=[jax.ShapeDtypeStruct(out.shape, out.dtype) for out in outs],
        in_specs=[vmem] * len(outs),
        out_specs=[vmem] * len(outs),
    )(*outs)
    block_out, grad_input, d_q, d_k, d_v, d_o, d_g, d_u, d_d, gains_sum = outs
    flat = jnp.concatenate([gains_sum[0], gains_sum[2, : 2 * HEAD_DIM], gains_sum[1]])
    own_gains = lax.dynamic_slice(flat, (place * count,), (count,))
    return (block_out, grad_input, d_q, d_k.T, d_v.T, d_o, d_g.T, d_u.T, d_d, own_gains)


def any_body(*arguments):
    tokens, w_query, key_weight, w_gate = (arguments[i] for i in (0, 4, 5, 8))
    ctx, shards = lax.axis_size("ctx"), lax.axis_size("shard")
    fits = w_query.shape[1] == HEAD_DIM and 2 * key_weight.shape[1] == HEAD_DIM
    fits = fits and lax.axis_size("rep") == 2 and shards == 4 and ctx == 4
    fits = fits and w_gate.shape[1] % 64 == 0 and tokens.shape[1] % 16 == 0
    fits = fits and tokens.shape[0] * tokens.shape[1] * ctx <= 512
    if fits:
        return whole_layer_body(*arguments)
    return body(*arguments)


def solution(mesh):
    in_specs = (
        P(("rep", "shard"), "ctx", None),
        P(("rep", "shard"), None),
        P(("rep", "shard"), None),
        P(("rep", "shard"), "ctx", None),
        P(None, ("shard", "ctx")),
        P(None, ("shard", "ctx")),
        P(None, ("shard", "ctx")),
        P(("shard", "ctx"), None),
        P(None, ("shard", "ctx")),
        P(None, ("shard", "ctx")),
        P(("shard", "ctx"), None),
        P(("shard", "ctx")),
    )
    out_specs = (
        P(("rep", "shard"), "ctx", None),
        P(("rep", "shard"), "ctx", None),
        P(None, ("shard", "ctx")),
        P(None, ("shard", "ctx")),
        P(None, ("shard", "ctx")),
        P(("shard", "ctx"), None),
        P(None, ("shard", "ctx")),
        P(None, ("shard", "ctx")),
        P(("shard", "ctx"), None),
        P(("shard", "ctx")),
    )
    return jax.shard_map(any_body, mesh=mesh, in_specs=in_specs, out_specs=out_specs, check_vma=False)
```
